512 devices in a mesh: sec: 2 (over core), lat: 4 (over z_hi), lon: 64 (over x, y, z_lo).
Axes of the slice: x: 4, y: 8, z: 8 (z_hi: 4, z_lo: 2; z = z_hi * 2 + z_lo), core: 2. Of those that a mesh axis runs over, the one named last changes fastest.
Arguments:
- adjoint: float32 [2, 4, 4, 128, 8192], P('sec', None, None, 'lat', 'lon'), may hold values from -6 to 6
- diffusivity: float32 [2, 4, 128, 8192], P('sec', None, 'lat', 'lon'), may hold values from 0.02 to 0.2
- velocity: float32 [2, 2, 4, 128, 8192], P('sec', None, None, 'lat', 'lon'), may hold values from -0.4 to 0.4
- sensitivity: float32 [2, 4, 4], P('sec'), may hold values from -3 to 3
- sea_mask: int32 [2, 128, 8192], P('sec', 'lat', 'lon'), may hold values 0 or 1
- coast_distance: int32 [2, 128, 8192], P('sec', 'lat', 'lon'), may hold values from 0 to 31
- send_cells: int32 [2, 4, 192, 1024], P('sec', 'lat', 'lon'), may hold values from 0 to 4095
- recv_slots: int32 [2, 4, 128, 8192], P('sec', None, 'lat', 'lon'), may hold values from 0 to 3071
- regrid_weight: float32 [2, 4, 128, 8192], P('sec', None, 'lat', 'lon'), may hold values from 0.1 to 0.5
Outputs:
- adjoint_out: float32 [2, 4, 4, 128, 8192], P('sec', None, None, 'lat', 'lon')
The draws below stay inside these ranges and needn't reach their ends.
Inputs may be any that keep to these rules, and one draw needn't show every extreme that they name: `send_cells`: a cell number of the sending tile. `recv_slots`: an entry of the 3072 received entries, source tile major, west source first.
All inputs are finite; a program needn't handle non-finite values. No bound on the sum of `sea_mask` on one device may be relied on, other than what follows from the above.
Results may differ from the reference program's by a relative error of at most 0.0003.
Values sent between devices are 32-bit elements; how exact they have to be, the bound alone decides.
No kernel may reach another device: no remote copies, remote signals or barrier semaphores. Data moves between devices by JAX's collectives and lax.ppermute only.
A program may use at most 64 MiB of HBM per device.

```python
import math
import jax
import jax.numpy as jnp

TLAT = 32
TLON = 128
LEV = 4
CAP = 1024
COMP = 4
TERMS = 4
STEPS = 2
NLAT = 128
NLON = 8192
N_LAT = 4
N_LON = 64


def set_ends(entries, rng, low, top_value):
    longest = entries.shape.index(max(entries.shape))
    spots = []
    for shift in (0, 1):
        where = [jax.random.randint(jax.random.fold_in(rng, axis), (), 0, length) for axis, length in enumerate(entries.shape)]
        where[longest] = (where[longest] + shift) % entries.shape[longest]
        spots.append(tuple(where))
    return entries.at[spots[0]].set(low).at[spots[1]].set(top_value)


def shard_levels(rng, dims, cuts, low, high):
    def one(axis_at, parts):
        draws = jax.random.uniform(jax.random.fold_in(jax.random.fold_in(rng, 6), axis_at), (parts,), jnp.float32, low / len(cuts), high / len(cuts))
        return jnp.repeat(jnp.exp(draws), dims[axis_at] // parts).reshape((-1,) + (1,) * (len(dims) - axis_at - 1))

    factor_of = one(*cuts[0])
    for cut in cuts[1:]:
        factor_of = factor_of * one(*cut)
    return factor_of


def centred(rng, extent, width, most, split=(), kind=jnp.bfloat16):
    result = jax.random.normal(rng, extent, jnp.float32) * width
    if len(split) > 0:
        result = shard_levels(rng, extent, split, -0.22, 0.18) * result
    return jnp.clip(result, min=-most, max=most).astype(kind)


def setup_inputs(seed: int = 0) -> dict:
    streams_of = jax.random.split(jax.random.key(seed), 10)
    return {
        "adjoint": centred(streams_of[0], (2, COMP, LEV, NLAT, NLON), 1.0, 6.0, ((0, 2), (3, 4), (4, 64)), jnp.float32),
        "diffusivity": jnp.clip(jnp.exp(math.log(0.2) - 2.3025851 * jax.random.uniform(streams_of[1], (2, LEV, NLAT, NLON), jnp.float32) ** shard_levels(streams_of[1], (2, LEV, NLAT, NLON), ((0, 2), (2, 4), (3, 64)), -0.2, 0.2)), 0.02, 0.2),
        "velocity": jnp.clip(jax.random.uniform(streams_of[2], (2, 2, LEV, NLAT, NLON), jnp.float32, -0.4, 0.4) * shard_levels(streams_of[2], (2, 2, LEV, NLAT, NLON), ((0, 2), (3, 4), (4, 64)), -0.4, 0.0), -0.4, 0.4),
        "sensitivity": centred(streams_of[3], (2, COMP, COMP), 0.5, 3.0, ((0, 2),), jnp.float32),
        "sea_mask": set_ends((jax.random.randint(streams_of[4], (2, NLAT, NLON), 0, 4) < 3).astype(jnp.int32), jax.random.fold_in(streams_of[4], 1), 0, 1),
        "coast_distance": set_ends(jax.random.randint(streams_of[5], (2, NLAT, NLON), 0, 32), jax.random.fold_in(streams_of[5], 1), 0, 31).astype(jnp.int32),
        "send_cells": set_ends(jax.random.randint(streams_of[6], (2, N_LAT, N_LON * 3, CAP), 0, TLAT * TLON), jax.random.fold_in(streams_of[6], 1), 0, (TLAT * TLON) - 1).astype(jnp.int32),
        "recv_slots": set_ends(jax.random.randint(streams_of[7], (2, TERMS, NLAT, NLON), 0, 3 * CAP), jax.random.fold_in(streams_of[7], 1), 0, (3 * CAP) - 1).astype(jnp.int32),
        "regrid_weight": jnp.clip(0.1 + 0.4 * jax.random.uniform(streams_of[8], (2, TERMS, NLAT, NLON), jnp.float32) ** shard_levels(streams_of[8], (2, TERMS, NLAT, NLON), ((0, 2), (2, 4), (3, 64)), -0.2, 0.2), 0.1, 0.5),
    }


def to_tiles(array):
    lead = array.shape[1]
    shaped = array.reshape(2, lead, N_LAT, TLAT, N_LON, TLON)
    return shaped.transpose(0, 2, 4, 1, 3, 5).reshape(2, N_LAT, N_LON, lead, TLAT * TLON)


def from_tiles(array):
    lead = array.shape[3]
    shaped = array.reshape(2, N_LAT, N_LON, lead, TLAT, TLON)
    return shaped.transpose(0, 3, 1, 4, 2, 5).reshape(2, lead, NLAT, NLON)


def pad_rims(array):
    wrapped = jnp.concatenate([array[..., -1:], array, array[..., :1]], axis=-1)
    widths = [(0, 0)] * (array.ndim - 2) + [(1, 1), (0, 0)]
    return jnp.pad(wrapped, widths)


def sweep_once(field, coef_padded):
    padded = pad_rims(field)
    diffused = coef_padded[:, 0:1] * padded
    carried_x = coef_padded[:, 1:2] * padded
    carried_y = coef_padded[:, 2:3] * padded
    centre = diffused[..., 1:-1, 1:-1]
    laplace = diffused[..., 2:, 1:-1] + diffused[..., :-2, 1:-1] + diffused[..., 1:-1, 2:] + diffused[..., 1:-1, :-2] - 4.0 * centre
    advect = 0.5 * (carried_x[..., 1:-1, 2:] - carried_x[..., 1:-1, :-2]) + 0.5 * (carried_y[..., 2:, 1:-1] - carried_y[..., :-2, 1:-1])
    return field + laplace + advect


def couple(field, sensitivity, weight_sea, send_cells, slot_tiles, weight_tiles):
    surface = field[:, :, 0]
    fluxes = []
    for which in range(COMP):
        total = jnp.zeros((2, NLAT, NLON), jnp.float32)
        for other in range(COMP):
            total = total + sensitivity[:, which, other][:, None, None] * surface[:, other]
        fluxes.append(weight_sea * total)
    flux = jnp.stack(fluxes, axis=1)
    flux_tiles = to_tiles(flux)
    index = send_cells.reshape(2, N_LAT, N_LON, 1, 3 * CAP).astype(jnp.int32)
    index = jnp.broadcast_to(index, (2, N_LAT, N_LON, COMP, 3 * CAP))
    packed = jnp.take_along_axis(flux_tiles, index, axis=4)
    packed = packed.reshape(2, N_LAT, N_LON, COMP, 3, CAP)
    other_side = packed[::-1]
    pieces = []
    for source in range(3):
        rolled = jnp.roll(other_side[:, :, :, :, 2 - source], -(source - 1), axis=2)
        pieces.append(rolled)
    received = jnp.concatenate(pieces, axis=4)
    total = jnp.zeros((2, N_LAT, N_LON, COMP, TLAT * TLON), jnp.float32)
    for which in range(TERMS):
        slots = jnp.broadcast_to(slot_tiles[:, :, :, which:which + 1], (2, N_LAT, N_LON, COMP, TLAT * TLON)).astype(jnp.int32)
        picked = jnp.take_along_axis(received, slots, axis=4)
        total = total + weight_tiles[:, :, :, which:which + 1] * picked
    return from_tiles(total)


def reference(adjoint, diffusivity, velocity, sensitivity, sea_mask, coast_distance, send_cells, recv_slots, regrid_weight):
    distance = coast_distance.astype(jnp.float32)
    blend = (distance + 1.0) / (distance + 9.0)
    weight_sea = sea_mask.astype(jnp.float32) * blend
    coefficients = jnp.concatenate([diffusivity[:, None], velocity], axis=1)
    coef_padded = pad_rims(coefficients)
    slot_tiles = to_tiles(recv_slots)
    weight_tiles = to_tiles(regrid_weight)
    field = adjoint
    for step_index in range(STEPS):
        coupled = couple(field, sensitivity, weight_sea, send_cells, slot_tiles, weight_tiles)
        field = sweep_once(field, coef_padded)
        field = field.at[:, :, 0].add(coupled)
    return field
```

```python
import functools

import jax
import jax.numpy as jnp
from jax import lax
from jax.experimental import pallas as pl
from jax.experimental.pallas import tpu as pltpu
from jax.sharding import PartitionSpec as P

COMP = 4
LEV = 4
TERMS = 4
ROWS = 32
LANES = 128
BLOCKS = ROWS // 8
PEERS = 3
PLANES = COMP * LEV

LIST = 8 * COMP
SIDE = LIST + 8
KEEP = SIDE + PLANES
GIVE = KEEP + LIST


def lookup(rows, high, low):
    found = [jnp.zeros((8, LANES), jnp.float32) for _ in rows]
    for at in range(len(rows[0])):
        here = high == at
        for k in range(len(rows)):
            row = jnp.broadcast_to(rows[k][at](), (8, LANES))
            got = jnp.take_along_axis(row, low, axis=1, mode="promise_in_bounds")
            found[k] = jnp.where(here, got, found[k])
    return found


def outgoing(core, field, dif_ref, vel_ref, sens_ref, sea_ref, dist_ref, send_ref, flux_ref, keep_ref, give_ref):
    distance = dist_ref[...].astype(jnp.float32)
    blend = (distance + 1.0) / (distance + 9.0)
    weight = sea_ref[...].astype(jnp.float32) * blend
    surface = [field(k, 0) for k in range(COMP)]
    for k in range(COMP):
        total = sens_ref[k, 0] * surface[0]
        for j in range(1, COMP):
            total = total + sens_ref[k, j] * surface[j]
        flux_ref[k] = weight * total

    first = core == 0
    cells = []
    for d in range(PEERS):
        pieces = [send_ref[d : d + 1, LANES * i : LANES * (i + 1)] for i in range(8)]
        cells.append(jnp.concatenate(pieces, axis=0))
    east_west = (jnp.where(first, cells[2], cells[0]), jnp.where(first, cells[0], cells[2]), cells[1])
    table = [[functools.partial(lambda k, r: flux_ref[k, r : r + 1, :], k, r) for r in range(ROWS)] for k in range(COMP)]
    for which, cell in enumerate(east_west):
        found = lookup(table, cell >> 7, cell & (LANES - 1))
        for k in range(COMP):
            if which == 0:
                keep_ref[8 * k : 8 * k + 8, :] = found[k]
            elif which == 1:
                give_ref[8 * k : 8 * k + 8, :] = found[k]
            else:
                give_ref[KEEP + 8 * k : KEEP + 8 * k + 8, :] = found[k]

    lane = lax.broadcasted_iota(jnp.int32, (8, LANES), 1)
    east = jnp.zeros((8, LANES), jnp.float32)
    west = jnp.zeros((8, LANES), jnp.float32)
    for level in range(LEV):
        dif = dif_ref[level]
        half_u = 0.5 * vel_ref[0, level]
        half_v = 0.5 * vel_ref[1, level]
        for k in range(COMP):
            plane = field(k, level)
            at = LEV * k + level
            to_east = (dif - half_u) * plane
            to_west = (dif + half_u) * plane
            for b in range(BLOCKS):
                here = lane == PLANES * b + at
                rows = slice(8 * b, 8 * b + 8)
                east = jnp.where(here, jnp.broadcast_to(to_east[rows, LANES - 1 :], (8, LANES)), east)
                west = jnp.where(here, jnp.broadcast_to(to_west[rows, :1], (8, LANES)), west)
            to_north = ((dif[24:] - half_v[24:]) * plane[24:])[7:8]
            to_south = ((dif[:8] + half_v[:8]) * plane[:8])[0:1]
            keep_ref[SIDE + at : SIDE + at + 1, :] = jnp.where(first, to_north, to_south)
            give_ref[SIDE + at : SIDE + at + 1, :] = jnp.where(first, to_south, to_north)
    keep_ref[LIST:SIDE, :] = jnp.where(first, east, west)
    give_ref[LIST:SIDE, :] = jnp.where(first, west, east)


def advance(core, field_ref, dif_ref, vel_ref, slot_ref, weight_ref, lon_ref, lat_ref, near_ref, back_ref, out_ref):
    first = core == 0
    def row_of(k, r):
        if r < 8:
            return lambda: lon_ref[SIDE + 8 * k + r : SIDE + 8 * k + r + 1, :]
        if r < 16:
            return lambda: near_ref[KEEP + 8 * k + r - 8 : KEEP + 8 * k + r - 7, :]
        return lambda: back_ref[8 * k + r - 16 : 8 * k + r - 15, :]

    table = [[row_of(k, r) for r in range(8 * PEERS)] for k in range(COMP)]
    kept_side = lon_ref[LIST:SIDE, :]
    passed_side = back_ref[LIST:SIDE, :]
    from_west = jnp.where(first, kept_side, passed_side)
    from_east = jnp.where(first, passed_side, kept_side)
    lane = lax.broadcasted_iota(jnp.int32, (8, LANES), 1)
    row = lax.broadcasted_iota(jnp.int32, (ROWS, LANES), 0)

    for level in range(LEV):
        dif = dif_ref[level]
        half_u = 0.5 * vel_ref[0, level]
        half_v = 0.5 * vel_ref[1, level]
        for k in range(COMP):
            at = LEV * k + level
            plane = field_ref[k, level]
            kept_row = lat_ref[at : at + 1, :]
            passed_row = back_ref[SIDE + at : SIDE + at + 1, :]
            south_row = jnp.where(first, kept_row, passed_row)
            north_row = jnp.where(first, passed_row, kept_row)
            east = pltpu.roll((dif + half_u) * plane, LANES - 1, 1)
            west = pltpu.roll((dif - half_u) * plane, 1, 1)
            north = pltpu.roll((dif + half_v) * plane, ROWS - 1, 0)
            south = pltpu.roll((dif - half_v) * plane, 1, 0)
            north = jnp.where(row == ROWS - 1, jnp.broadcast_to(north_row, (ROWS, LANES)), north)
            south = jnp.where(row == 0, jnp.broadcast_to(south_row, (ROWS, LANES)), south)
            centre = plane - 4.0 * (dif * plane) + (north + south)
            for b in range(BLOCKS):
                rows = slice(8 * b, 8 * b + 8)
                j = PLANES * b + at
                edge_east = jnp.broadcast_to(from_east[:, j : j + 1], (8, LANES))
                edge_west = jnp.broadcast_to(from_west[:, j : j + 1], (8, LANES))
                across = jnp.where(lane == LANES - 1, edge_east, east[rows]) + jnp.where(lane == 0, edge_west, west[rows])
                out_ref[k, level, rows, :] = centre[rows] + across

    for b in range(BLOCKS):
        rows = slice(8 * b, 8 * b + 8)
        total = [jnp.zeros((8, LANES), jnp.float32) for _ in range(COMP)]
        for t in range(TERMS):
            slot = slot_ref[t, rows, :]
            source = slot >> 10
            source = jnp.where(first, source, 2 - source)
            high = source * 8 + ((slot >> 7) & 7)
            found = lookup(table, high, slot & (LANES - 1))
            for k in range(COMP):
                total[k] = total[k] + weight_ref[t, rows, :] * found[k]
        for k in range(COMP):
            out_ref[k, 0, rows, :] = out_ref[k, 0, rows, :] + total[k]


def start_kernel(core_ref, sens_ref, field_ref, dif_ref, vel_ref, sea_ref, dist_ref, send_ref, keep_ref, give_ref, flux_ref):
    outgoing(
        core_ref[0], lambda k, l: field_ref[k, l], dif_ref, vel_ref, sens_ref, sea_ref, dist_ref, send_ref, flux_ref, keep_ref, give_ref
    )


def middle_kernel(
    core_ref, sens_ref, field_ref, dif_ref, vel_ref, sea_ref, dist_ref, send_ref, slot_ref, weight_ref,
    lon_ref, lat_ref, near_ref, back_ref, out_ref, keep_ref, give_ref, flux_ref,
):
    core = core_ref[0]
    advance(core, field_ref, dif_ref, vel_ref, slot_ref, weight_ref, lon_ref, lat_ref, near_ref, back_ref, out_ref)
    outgoing(
        core, lambda k, l: out_ref[k, l], dif_ref, vel_ref, sens_ref, sea_ref, dist_ref, send_ref, flux_ref, keep_ref, give_ref
    )


def last_kernel(
    core_ref, field_ref, dif_ref, vel_ref, slot_ref, weight_ref, lon_ref, lat_ref, near_ref, back_ref, out_ref
):
    advance(core_ref[0], field_ref, dif_ref, vel_ref, slot_ref, weight_ref, lon_ref, lat_ref, near_ref, back_ref, out_ref)


def call(kernel, scalars, arrays, outs, scratch=()):
    in_vmem = pl.BlockSpec(memory_space=pltpu.VMEM)
    in_smem = pl.BlockSpec(memory_space=pltpu.SMEM)
    return pl.pallas_call(
        kernel,
        out_shape=[jax.ShapeDtypeStruct(shape, jnp.float32) for shape in outs],
        in_specs=[in_smem] * len(scalars) + [in_vmem] * len(arrays),
        out_specs=[in_vmem] * len(outs),
        scratch_shapes=[pltpu.VMEM(shape, jnp.float32) for shape in scratch],
        compiler_params=pltpu.CompilerParams(vmem_limit_bytes=8 << 20),
    )(*scalars, *arrays)


def routes(axis):
    count = lax.axis_size(axis)
    periodic = axis == "lon"
    pairs = []
    for i in range(count):
        if periodic or i + 1 < count:
            pairs.append((i, (i + 1) % count))
        if periodic or i > 0:
            pairs.append((count + i, count + (i - 1) % count))
    return pairs


def exchange(keep, give):
    near = lax.ppermute(give, "sec", [(0, 1), (1, 0)])
    lon = jnp.concatenate([keep[:SIDE], near[:SIDE]], axis=0)
    lat = jnp.concatenate([keep[SIDE:], near[SIDE:KEEP]], axis=0)
    lon = lax.ppermute(lon, ("sec", "lon"), routes("lon"))
    lat = lax.ppermute(lat, ("sec", "lat"), routes("lat"))
    back = jnp.concatenate([lon[:LIST], lon[SIDE + LIST :], lat[PLANES:]], axis=0)
    back = lax.ppermute(back, "sec", [(0, 1), (1, 0)])
    return lon, lat, near, back


def on_device(
    adjoint,
    diffusivity,
    velocity,
    sensitivity,
    sea_mask,
    coast_distance,
    send_cells,
    recv_slots,
    regrid_weight,
):
    core = lax.axis_index("sec").astype(jnp.int32).reshape(1)
    field = adjoint[0]
    sens = sensitivity[0]
    dif, vel = diffusivity[0], velocity[0]
    send = (sea_mask[0], coast_distance[0], send_cells[0, 0])
    take = (recv_slots[0], regrid_weight[0])
    shape = field.shape
    flux = [(COMP, ROWS, LANES)]
    messages = [(KEEP, LANES), (GIVE, LANES)]
    keep, give = call(start_kernel, (core, sens), (field, dif, vel, *send), messages, flux)
    arrived = exchange(keep, give)
    field, keep, give = call(
        middle_kernel, (core, sens), (field, dif, vel, *send, *take, *arrived), [shape] + messages, flux
    )
    arrived = exchange(keep, give)
    (field,) = call(last_kernel, (core,), (field, dif, vel, *take, *arrived), [shape])
    return field[None]


def solution(mesh):
    placed = (
        P("sec", None, None, "lat", "lon"),
        P("sec", None, "lat", "lon"),
        P("sec", None, None, "lat", "lon"),
        P("sec", None, None),
        P("sec", "lat", "lon"),
        P("sec", "lat", "lon"),
        P("sec", "lat", "lon", None),
        P("sec", None, "lat", "lon"),
        P("sec", None, "lat", "lon"),
    )
    return jax.shard_map(
        on_device,
        mesh=mesh,
        in_specs=placed,
        out_specs=P("sec", None, None, "lat", "lon"),
        check_vma=False,
    )
```

```python
import jax
import jax.numpy as jnp
from jax import lax
from jax.experimental import pallas as pl
from jax.experimental.pallas import tpu as pltpu
from jax.sharding import PartitionSpec as P

COMP = 4
LEV = 4
TERMS = 4
ROWS = 32
LANES = 128
BLOCKS = ROWS // 8
PEERS = 3
PLANES = COMP * LEV

LIST = 8 * COMP
SIDE = LIST + 8
KEEP = SIDE + PLANES
GIVE = KEEP + LIST


def lookup(rows, high, low, first_row):
    found = [jnp.zeros((8, LANES), jnp.float32) for _ in range(COMP)]
    for r in range(len(rows[0])):
        here = high == first_row + r
        for k in range(COMP):
            row = jnp.broadcast_to(rows[k][r](), (8, LANES))
            got = jnp.take_along_axis(row, low, axis=1, mode="promise_in_bounds")
            found[k] = jnp.where(here, got, found[k])
    return found


def regrid(list_ref, offset, source, slot_ref, weight_ref, b):
    rows = slice(8 * b, 8 * b + 8)

    def row_of(k, r):
        at = offset + 8 * k + r
        return lambda: list_ref[at : at + 1, :]

    table = [[row_of(k, r) for r in range(8)] for k in range(COMP)]
    total = None
    for t in range(TERMS):
        slot = slot_ref[t, rows, :]
        found = lookup(table, slot >> 7, slot & (LANES - 1), 8 * source)
        found = [weight_ref[t, rows, :] * entry for entry in found]
        total = found if total is None else [a + b for a, b in zip(total, found)]
    return total


def outgoing(core, field, dif_ref, vel_ref, sens_ref, weight, cells, flux_ref, keep_ref, give_ref, ready):
    surface = [field(k, 0) for k in range(COMP)]
    for k in range(COMP):
        total = sens_ref[k : k + 1, 0:1] * surface[0]
        for j in range(1, COMP):
            total = total + sens_ref[k : k + 1, j : j + 1] * surface[j]
        flux_ref[k] = weight * total

    first = core == 0
    kept = jnp.where(first, cells[2], cells[0])
    given = jnp.where(first, cells[0], cells[2])

    def row_of(k, r):
        return lambda: flux_ref[k, r : r + 1, :]

    table = [[row_of(k, r) for r in range(ROWS)] for k in range(COMP)]
    for cell, ref, offset in ((kept, keep_ref, 0), (given, give_ref, 0), (cells[1], give_ref, KEEP)):
        found = lookup(table, cell >> 7, cell & (LANES - 1), 0)
        for k in range(COMP):
            ref[offset + 8 * k : offset + 8 * k + 8, :] = found[k]

    ready()
    lane = lax.broadcasted_iota(jnp.int32, (8, LANES), 1)
    east = jnp.zeros((8, LANES), jnp.float32)
    west = jnp.zeros((8, LANES), jnp.float32)
    for level in range(LEV):
        dif = dif_ref[level]
        half_u = 0.5 * vel_ref[0, level]
        half_v = 0.5 * vel_ref[1, level]
        for k in range(COMP):
            plane = field(k, level)
            at = LEV * k + level
            to_east = (dif - half_u) * plane
            to_west = (dif + half_u) * plane
            for b in range(BLOCKS):
                here = lane == PLANES * b + at
                rows = slice(8 * b, 8 * b + 8)
                east = jnp.where(here, jnp.broadcast_to(to_east[rows, LANES - 1 :], (8, LANES)), east)
                west = jnp.where(here, jnp.broadcast_to(to_west[rows, :1], (8, LANES)), west)
            to_north = ((dif[24:] - half_v[24:]) * plane[24:])[7:8]
            to_south = ((dif[:8] + half_v[:8]) * plane[:8])[0:1]
            keep_ref[SIDE + at : SIDE + at + 1, :] = jnp.where(first, to_north, to_south)
            give_ref[SIDE + at : SIDE + at + 1, :] = jnp.where(first, to_south, to_north)
    keep_ref[LIST:SIDE, :] = jnp.where(first, east, west)
    give_ref[LIST:SIDE, :] = jnp.where(first, west, east)


def weight_and_cells(sea_ref, dist_ref, send_ref):
    distance = dist_ref[...].astype(jnp.float32)
    blend = (distance + 1.0) / (distance + 9.0)
    return sea_ref[...].astype(jnp.float32) * blend, [send_ref[8 * d : 8 * d + 8, :] for d in range(PEERS)]


def start_kernel(
    sens_hbm, field_hbm, dif_hbm, vel_hbm, sea_hbm, dist_hbm, send_hbm,
    keep_ref, give_ref, flux_ref, sens_ref, field_ref, dif_ref, vel_ref, sea_ref, dist_ref, send_ref, sems,
):
    early = [(sens_hbm, sens_ref), (send_hbm, send_ref), (sea_hbm, sea_ref), (dist_hbm, dist_ref)]
    early += [(field_hbm.at[k, 0], field_ref.at[k, 0]) for k in range(COMP)]
    late = [(dif_hbm, dif_ref), (vel_hbm, vel_ref)]
    late += [(field_hbm.at[k, pl.ds(1, LEV - 1)], field_ref.at[k, pl.ds(1, LEV - 1)]) for k in range(COMP)]
    copies = [pltpu.make_async_copy(a, b, sems.at[i]) for i, (a, b) in enumerate(early + late)]
    for copy in copies:
        copy.start()
    for copy in copies[: len(early)]:
        copy.wait()

    def ready():
        for copy in copies[len(early) :]:
            copy.wait()

    weight, cells = weight_and_cells(sea_ref, dist_ref, send_ref)
    outgoing(
        lax.axis_index("sec"), lambda k, l: field_ref[k, l], dif_ref, vel_ref, sens_ref, weight, cells, flux_ref, keep_ref, give_ref, ready
    )


def inner_kernel(field_ref, dif_ref, vel_ref, slot_ref, weight_ref, near_ref, base_ref):
    lane = lax.broadcasted_iota(jnp.int32, (ROWS, LANES), 1)
    row = lax.broadcasted_iota(jnp.int32, (ROWS, LANES), 0)
    for level in range(LEV):
        dif = dif_ref[level]
        half_u = 0.5 * vel_ref[0, level]
        half_v = 0.5 * vel_ref[1, level]
        for k in range(COMP):
            plane = field_ref[k, level]
            east = jnp.where(lane == LANES - 1, 0.0, pltpu.roll((dif + half_u) * plane, LANES - 1, 1))
            west = jnp.where(lane == 0, 0.0, pltpu.roll((dif - half_u) * plane, 1, 1))
            north = jnp.where(row == ROWS - 1, 0.0, pltpu.roll((dif + half_v) * plane, ROWS - 1, 0))
            south = jnp.where(row == 0, 0.0, pltpu.roll((dif - half_v) * plane, 1, 0))
            base_ref[k, level] = plane - 4.0 * (dif * plane) + ((north + south) + (east + west))
    for b in range(BLOCKS):
        rows = slice(8 * b, 8 * b + 8)
        total = regrid(near_ref, KEEP, 1, slot_ref, weight_ref, b)
        for k in range(COMP):
            base_ref[k, 0, rows, :] = base_ref[k, 0, rows, :] + total[k]


def kept_kernel(slot_ref, weight_ref, lon_ref, part_ref):
    source = 2 * lax.axis_index("sec")
    for b in range(BLOCKS):
        total = regrid(lon_ref, SIDE, source, slot_ref, weight_ref, b)
        for k in range(COMP):
            part_ref[k, 8 * b : 8 * b + 8, :] = total[k]


def finish(core, base_ref, part_ref, slot_ref, weight_ref, edge_ref, back_ref, out_ref):
    first = core == 0
    kept_side = edge_ref[:8, :]
    passed_side = back_ref[LIST:SIDE, :]
    from_west = jnp.where(first, kept_side, passed_side)
    from_east = jnp.where(first, passed_side, kept_side)
    lane = lax.broadcasted_iota(jnp.int32, (8, LANES), 1)
    row = lax.broadcasted_iota(jnp.int32, (8, LANES), 0)
    for b in range(BLOCKS):
        rows = slice(8 * b, 8 * b + 8)
        total = regrid(back_ref, 0, 2 - 2 * core, slot_ref, weight_ref, b)
        for level in range(LEV):
            for k in range(COMP):
                at = LEV * k + level
                j = PLANES * b + at
                edge_east = jnp.broadcast_to(from_east[:, j : j + 1], (8, LANES))
                edge_west = jnp.broadcast_to(from_west[:, j : j + 1], (8, LANES))
                edge = jnp.where(lane == LANES - 1, edge_east, jnp.where(lane == 0, edge_west, 0.0))
                if b == 0 or b == BLOCKS - 1:
                    kept_row = edge_ref[8 + at : 9 + at, :]
                    passed_row = back_ref[SIDE + at : SIDE + at + 1, :]
                    pair = (kept_row, passed_row) if b == 0 else (passed_row, kept_row)
                    end = jnp.broadcast_to(jnp.where(first, *pair), (8, LANES))
                    edge = edge + jnp.where(row == (0 if b == 0 else 7), end, 0.0)
                value = base_ref[k, level, rows, :] + edge
                if level == 0:
                    value = value + (part_ref[k, rows, :] + total[k])
                out_ref[k, level, rows, :] = value


def middle_kernel(
    sens_ref, base_ref, part_ref, slot_ref, weight_ref, edge_ref, back_ref, dif_ref, vel_ref, sea_ref, dist_ref, send_ref,
    out_ref, keep_ref, give_ref, flux_ref,
):
    core = lax.axis_index("sec")
    finish(core, base_ref, part_ref, slot_ref, weight_ref, edge_ref, back_ref, out_ref)
    weight, cells = weight_and_cells(sea_ref, dist_ref, send_ref)
    outgoing(
        core, lambda k, l: out_ref[k, l], dif_ref, vel_ref, sens_ref, weight, cells, flux_ref, keep_ref, give_ref, lambda: None
    )


def last_kernel(base_ref, part_ref, slot_ref, weight_ref, edge_ref, back_ref, out_ref):
    finish(lax.axis_index("sec"), base_ref, part_ref, slot_ref, weight_ref, edge_ref, back_ref, out_ref)


def call(kernel, arrays, outs, scratch=(), space=pltpu.VMEM, cost=1 << 20):
    in_space = pl.BlockSpec(memory_space=space)
    in_vmem = pl.BlockSpec(memory_space=pltpu.VMEM)
    return pl.pallas_call(
        kernel,
        out_shape=[jax.ShapeDtypeStruct(shape, jnp.float32) for shape in outs],
        in_specs=[in_space] * len(arrays),
        out_specs=[in_vmem] * len(outs),
        scratch_shapes=list(scratch),
        compiler_params=pltpu.CompilerParams(vmem_limit_bytes=8 << 20),
        cost_estimate=pl.CostEstimate(flops=cost, transcendentals=0, bytes_accessed=cost),
    )(*arrays)


def routes(axis):
    count = lax.axis_size(axis)
    periodic = axis == "lon"
    pairs = []
    for i in range(count):
        if periodic or i + 1 < count:
            pairs.append((i, (i + 1) % count))
        if periodic or i > 0:
            pairs.append((count + i, count + (i - 1) % count))
    return pairs


def step(keep, give, field, dif, vel, take):
    near = lax.ppermute(give, "sec", [(0, 1), (1, 0)])
    lon = jnp.concatenate([keep[:SIDE], near[:SIDE]], axis=0)
    lat = jnp.concatenate([keep[SIDE:], near[SIDE:KEEP]], axis=0)
    lon = lax.ppermute(lon, ("sec", "lon"), routes("lon"))
    lat = lax.ppermute(lat, ("sec", "lat"), routes("lat"))
    (base,) = call(inner_kernel, (field, dif, vel, *take, near), [field.shape])
    back = jnp.concatenate([lon[:LIST], lon[SIDE + LIST :], lat[PLANES:]], axis=0)
    back = lax.ppermute(back, "sec", [(0, 1), (1, 0)])
    (part,) = call(kept_kernel, (*take, lon), [(COMP, ROWS, LANES)])
    edge = jnp.concatenate([lon[LIST:SIDE], lat[:PLANES]], axis=0)
    return base, part, *take, edge, back


def on_device(
    adjoint,
    diffusivity,
    velocity,
    sensitivity,
    sea_mask,
    coast_distance,
    send_cells,
    recv_slots,
    regrid_weight,
):
    field = adjoint[0]
    sens = sensitivity[0]
    dif, vel = diffusivity[0], velocity[0]
    send = (sea_mask[0], coast_distance[0], send_cells.reshape(8 * PEERS, LANES))
    take = (recv_slots[0], regrid_weight[0])
    messages = [(KEEP, LANES), (GIVE, LANES)]
    flux = pltpu.VMEM((COMP, ROWS, LANES), jnp.float32)
    held = [pltpu.VMEM(a.shape, a.dtype) for a in (sens, field, dif, vel, *send)]
    sems = pltpu.SemaphoreType.DMA((6 + 2 * COMP,))
    fresh = [pltpu.with_memory_space_constraint(a, pltpu.HBM) for a in (sens, field, dif, vel, *send)]
    keep, give = call(start_kernel, fresh, messages, [flux, *held, sems], pltpu.HBM)
    state = step(keep, give, field, dif, vel, take)
    field, keep, give = call(
        middle_kernel, (sens, *state, dif, vel, *send), [field.shape] + messages, [flux]
    )
    state = step(keep, give, field, dif, vel, take)
    (field,) = call(last_kernel, state, [field.shape])
    return field[None]


def solution(mesh):
    placed = (
        P("sec", None, None, "lat", "lon"),
        P("sec", None, "lat", "lon"),
        P("sec", None, None, "lat", "lon"),
        P("sec", None, None),
        P("sec", "lat", "lon"),
        P("sec", "lat", "lon"),
        P("sec", "lat", "lon", None),
        P("sec", None, "lat", "lon"),
        P("sec", None, "lat", "lon"),
    )
    return jax.shard_map(
        on_device,
        mesh=mesh,
        in_specs=placed,
        out_specs=P("sec", None, None, "lat", "lon"),
        check_vma=False,
    )
```

```python
import jax
import jax.numpy as jnp
from jax import lax
from jax.experimental import pallas as pl
from jax.experimental.pallas import tpu as pltpu
from jax.sharding import PartitionSpec as P

COMP = 4
LEV = 4
TERMS = 4
ROWS = 32
LANES = 128
BLOCKS = ROWS // 8
PEERS = 3
PLANES = COMP * LEV

LIST = 8 * COMP
SIDE = LIST + 8
KEEP = SIDE + PLANES
GIVE = KEEP + LIST


def lookup(rows, high, low, first_row):
    found = [jnp.zeros((8, LANES), jnp.float32) for _ in range(COMP)]
    for r in range(len(rows[0])):
        here = high == first_row + r
        for k in range(COMP):
            row = jnp.broadcast_to(rows[k][r](), (8, LANES))
            got = jnp.take_along_axis(row, low, axis=1, mode="promise_in_bounds")
            found[k] = jnp.where(here, got, found[k])
    return found


def regrid(list_ref, offset, source, slot_ref, weight_ref, b):
    rows = slice(8 * b, 8 * b + 8)

    def row_of(k, r):
        at = offset + 8 * k + r
        return lambda: list_ref[at : at + 1, :]

    table = [[row_of(k, r) for r in range(8)] for k in range(COMP)]
    total = None
    for t in range(TERMS):
        slot = slot_ref[t, rows, :]
        found = lookup(table, slot >> 7, slot & (LANES - 1), 8 * source)
        found = [weight_ref[t, rows, :] * entry for entry in found]
        total = found if total is None else [a + b for a, b in zip(total, found)]
    return total


def outgoing(core, field, dif_ref, vel_ref, sens_ref, weight, cells, flux_ref, keep_ref, give_ref, ready):
    surface = [field(k, 0) for k in range(COMP)]
    for k in range(COMP):
        total = sens_ref[k : k + 1, 0:1] * surface[0]
        for j in range(1, COMP):
            total = total + sens_ref[k : k + 1, j : j + 1] * surface[j]
        flux_ref[k] = weight * total

    first = core == 0
    kept = jnp.where(first, cells[2], cells[0])
    given = jnp.where(first, cells[0], cells[2])

    def row_of(k, r):
        return lambda: flux_ref[k, r : r + 1, :]

    table = [[row_of(k, r) for r in range(ROWS)] for k in range(COMP)]
    for cell, ref, offset in ((kept, keep_ref, 0), (given, give_ref, 0), (cells[1], give_ref, KEEP)):
        found = lookup(table, cell >> 7, cell & (LANES - 1), 0)
        for k in range(COMP):
            ref[offset + 8 * k : offset + 8 * k + 8, :] = found[k]

    ready()
    lane = lax.broadcasted_iota(jnp.int32, (8, LANES), 1)
    east = jnp.zeros((8, LANES), jnp.float32)
    west = jnp.zeros((8, LANES), jnp.float32)
    for level in range(LEV):
        dif = dif_ref[level]
        half_u = 0.5 * vel_ref[0, level]
        half_v = 0.5 * vel_ref[1, level]
        for k in range(COMP):
            plane = field(k, level)
            at = LEV * k + level
            to_east = (dif - half_u) * plane
            to_west = (dif + half_u) * plane
            for b in range(BLOCKS):
                here = lane == PLANES * b + at
                rows = slice(8 * b, 8 * b + 8)
                east = jnp.where(here, jnp.broadcast_to(to_east[rows, LANES - 1 :], (8, LANES)), east)
                west = jnp.where(here, jnp.broadcast_to(to_west[rows, :1], (8, LANES)), west)
            to_north = ((dif[24:] - half_v[24:]) * plane[24:])[7:8]
            to_south = ((dif[:8] + half_v[:8]) * plane[:8])[0:1]
            keep_ref[SIDE + at : SIDE + at + 1, :] = jnp.where(first, to_north, to_south)
            give_ref[SIDE + at : SIDE + at + 1, :] = jnp.where(first, to_south, to_north)
    keep_ref[LIST:SIDE, :] = jnp.where(first, east, west)
    give_ref[LIST:SIDE, :] = jnp.where(first, west, east)


def weight_and_cells(sea_ref, dist_ref, send_ref):
    distance = dist_ref[...].astype(jnp.float32)
    blend = (distance + 1.0) / (distance + 9.0)
    return sea_ref[...].astype(jnp.float32) * blend, [send_ref[8 * d : 8 * d + 8, :] for d in range(PEERS)]


def start_kernel(
    sens_hbm, field_hbm, dif_hbm, vel_hbm, sea_hbm, dist_hbm, send_hbm,
    keep_ref, give_ref, flux_ref, sens_ref, field_ref, dif_ref, vel_ref, sea_ref, dist_ref, send_ref, sems,
):
    early = [(sens_hbm, sens_ref), (send_hbm, send_ref), (sea_hbm, sea_ref), (dist_hbm, dist_ref)]
    early += [(field_hbm.at[k, 0], field_ref.at[k, 0]) for k in range(COMP)]
    late = [(dif_hbm, dif_ref), (vel_hbm, vel_ref)]
    late += [(field_hbm.at[k, pl.ds(1, LEV - 1)], field_ref.at[k, pl.ds(1, LEV - 1)]) for k in range(COMP)]
    copies = [pltpu.make_async_copy(a, b, sems.at[i]) for i, (a, b) in enumerate(early + late)]
    for copy in copies:
        copy.start()
    for copy in copies[: len(early)]:
        copy.wait()

    def ready():
        for copy in copies[len(early) :]:
            copy.wait()

    weight, cells = weight_and_cells(sea_ref, dist_ref, send_ref)
    outgoing(
        lax.axis_index("sec"), lambda k, l: field_ref[k, l], dif_ref, vel_ref, sens_ref, weight, cells, flux_ref, keep_ref, give_ref, ready
    )


def inner_kernel(field_ref, dif_ref, vel_ref, slot_ref, weight_ref, near_ref, base_ref):
    lane = lax.broadcasted_iota(jnp.int32, (ROWS, LANES), 1)
    row = lax.broadcasted_iota(jnp.int32, (ROWS, LANES), 0)
    for level in range(LEV):
        dif = dif_ref[level]
        half_u = 0.5 * vel_ref[0, level]
        half_v = 0.5 * vel_ref[1, level]
        for k in range(COMP):
            plane = field_ref[k, level]
            east = jnp.where(lane == LANES - 1, 0.0, pltpu.roll((dif + half_u) * plane, LANES - 1, 1))
            west = jnp.where(lane == 0, 0.0, pltpu.roll((dif - half_u) * plane, 1, 1))
            north = jnp.where(row == ROWS - 1, 0.0, pltpu.roll((dif + half_v) * plane, ROWS - 1, 0))
            south = jnp.where(row == 0, 0.0, pltpu.roll((dif - half_v) * plane, 1, 0))
            base_ref[k, level] = plane - 4.0 * (dif * plane) + ((north + south) + (east + west))
    for b in range(BLOCKS):
        rows = slice(8 * b, 8 * b + 8)
        total = regrid(near_ref, KEEP, 1, slot_ref, weight_ref, b)
        for k in range(COMP):
            base_ref[k, 0, rows, :] = base_ref[k, 0, rows, :] + total[k]


def kept_kernel(slot_ref, weight_ref, lon_ref, part_ref):
    source = 2 * lax.axis_index("sec")
    for b in range(BLOCKS):
        total = regrid(lon_ref, SIDE, source, slot_ref, weight_ref, b)
        for k in range(COMP):
            part_ref[k, 8 * b : 8 * b + 8, :] = total[k]


def finish(core, base_ref, part_ref, slot_ref, weight_ref, edge_ref, back_ref, out_ref):
    first = core == 0
    kept_side = edge_ref[:8, :]
    passed_side = back_ref[LIST:SIDE, :]
    from_west = jnp.where(first, kept_side, passed_side)
    from_east = jnp.where(first, passed_side, kept_side)
    lane = lax.broadcasted_iota(jnp.int32, (8, LANES), 1)
    row = lax.broadcasted_iota(jnp.int32, (8, LANES), 0)
    for b in range(BLOCKS):
        rows = slice(8 * b, 8 * b + 8)
        total = regrid(back_ref, 0, 2 - 2 * core, slot_ref, weight_ref, b)
        for level in range(LEV):
            for k in range(COMP):
                at = LEV * k + level
                j = PLANES * b + at
                edge_east = jnp.broadcast_to(from_east[:, j : j + 1], (8, LANES))
                edge_west = jnp.broadcast_to(from_west[:, j : j + 1], (8, LANES))
                edge = jnp.where(lane == LANES - 1, edge_east, jnp.where(lane == 0, edge_west, 0.0))
                if b == 0 or b == BLOCKS - 1:
                    kept_row = edge_ref[8 + at : 9 + at, :]
                    passed_row = back_ref[SIDE + at : SIDE + at + 1, :]
                    pair = (kept_row, passed_row) if b == 0 else (passed_row, kept_row)
                    end = jnp.broadcast_to(jnp.where(first, *pair), (8, LANES))
                    edge = edge + jnp.where(row == (0 if b == 0 else 7), end, 0.0)
                value = base_ref[k, level, rows, :] + edge
                if level == 0:
                    value = value + (part_ref[k, rows, :] + total[k])
                out_ref[k, level, rows, :] = value


def middle_kernel(
    sens_ref, base_ref, part_ref, slot_ref, weight_ref, edge_ref, back_ref, dif_ref, vel_ref, sea_ref, dist_ref, send_ref,
    out_ref, keep_ref, give_ref, flux_ref,
):
    core = lax.axis_index("sec")
    finish(core, base_ref, part_ref, slot_ref, weight_ref, edge_ref, back_ref, out_ref)
    weight, cells = weight_and_cells(sea_ref, dist_ref, send_ref)
    outgoing(
        core, lambda k, l: out_ref[k, l], dif_ref, vel_ref, sens_ref, weight, cells, flux_ref, keep_ref, give_ref, lambda: None
    )


def last_kernel(base_ref, part_ref, slot_ref, weight_ref, edge_ref, back_ref, out_ref):
    finish(lax.axis_index("sec"), base_ref, part_ref, slot_ref, weight_ref, edge_ref, back_ref, out_ref)


def call(kernel, arrays, outs, scratch=(), space=pltpu.VMEM, cost=1 << 20):
    in_space = pl.BlockSpec(memory_space=space)
    in_vmem = pl.BlockSpec(memory_space=pltpu.VMEM)
    return pl.pallas_call(
        kernel,
        out_shape=[jax.ShapeDtypeStruct(shape, jnp.float32) for shape in outs],
        in_specs=[in_space] * len(arrays),
        out_specs=[in_vmem] * len(outs),
        scratch_shapes=list(scratch),
        compiler_params=pltpu.CompilerParams(vmem_limit_bytes=8 << 20),
        cost_estimate=pl.CostEstimate(flops=cost, transcendentals=0, bytes_accessed=cost),
    )(*arrays)


def routes(axis):
    count = lax.axis_size(axis)
    periodic = axis == "lon"
    pairs = []
    for i in range(count):
        if periodic or i + 1 < count:
            pairs.append((i, (i + 1) % count))
        if periodic or i > 0:
            pairs.append((count + i, count + (i - 1) % count))
    return pairs


def step(keep, give, field, dif, vel, take):
    near = lax.ppermute(give, "sec", [(0, 1), (1, 0)])
    lon = jnp.concatenate([keep[:SIDE], near[:SIDE]], axis=0)
    fill = jnp.zeros((2 * (SIDE - PLANES), LANES), jnp.float32)
    lat = jnp.concatenate([keep[SIDE:], near[SIDE:KEEP], fill], axis=0)
    lon = lax.ppermute(lon, ("sec", "lon"), routes("lon"))
    lat = lax.ppermute(lat, ("sec", "lat"), routes("lat"))
    (base,) = call(inner_kernel, (field, dif, vel, *take, near), [field.shape])
    back = jnp.concatenate([lon[:LIST], lon[SIDE + LIST :], lat[PLANES : 2 * PLANES]], axis=0)
    back = lax.ppermute(back, "sec", [(0, 1), (1, 0)])
    (part,) = call(kept_kernel, (*take, lon), [(COMP, ROWS, LANES)])
    edge = jnp.concatenate([lon[LIST:SIDE], lat[:PLANES]], axis=0)
    return base, part, *take, edge, back


def on_device(
    adjoint,
    diffusivity,
    velocity,
    sensitivity,
    sea_mask,
    coast_distance,
    send_cells,
    recv_slots,
    regrid_weight,
):
    field = adjoint[0]
    sens = sensitivity[0]
    dif, vel = diffusivity[0], velocity[0]
    send = (sea_mask[0], coast_distance[0], send_cells.reshape(8 * PEERS, LANES))
    take = (recv_slots[0], regrid_weight[0])
    messages = [(KEEP, LANES), (GIVE, LANES)]
    flux = pltpu.VMEM((COMP, ROWS, LANES), jnp.float32)
    held = [pltpu.VMEM(a.shape, a.dtype) for a in (sens, field, dif, vel, *send)]
    sems = pltpu.SemaphoreType.DMA((6 + 2 * COMP,))
    fresh = [pltpu.with_memory_space_constraint(a, pltpu.HBM) for a in (sens, field, dif, vel, *send)]
    keep, give = call(start_kernel, fresh, messages, [flux, *held, sems], pltpu.HBM)
    state = step(keep, give, field, dif, vel, take)
    field, keep, give = call(
        middle_kernel, (sens, *state, dif, vel, *send), [field.shape] + messages, [flux]
    )
    state = step(keep, give, field, dif, vel, take)
    (field,) = call(last_kernel, state, [field.shape])
    return field[None]


def solution(mesh):
    placed = (
        P("sec", None, None, "lat", "lon"),
        P("sec", None, "lat", "lon"),
        P("sec", None, None, "lat", "lon"),
        P("sec", None, None),
        P("sec", "lat", "lon"),
        P("sec", "lat", "lon"),
        P("sec", "lat", "lon", None),
        P("sec", None, "lat", "lon"),
        P("sec", None, "lat", "lon"),
    )
    return jax.shard_map(
        on_device,
        mesh=mesh,
        in_specs=placed,
        out_specs=P("sec", None, None, "lat", "lon"),
        check_vma=False,
    )
```

```python
import jax
import jax.numpy as jnp
from jax import lax
from jax.experimental import pallas as pl
from jax.experimental.pallas import tpu as pltpu
from jax.sharding import PartitionSpec as P

COMP = 4
LEV = 4
TERMS = 4
ROWS = 32
LANES = 128
BLOCKS = ROWS // 8
PEERS = 3
PLANES = COMP * LEV

LIST = 8 * COMP
SIDE = LIST + 8
KEEP = SIDE + PLANES
GIVE = KEEP + LIST


def lookup(rows, high, low, first_row):
    found = [jnp.zeros((8, LANES), jnp.float32) for _ in range(COMP)]
    for r in range(len(rows[0])):
        here = high == first_row + r
        for k in range(COMP):
            row = jnp.broadcast_to(rows[k][r](), (8, LANES))
            got = jnp.take_along_axis(row, low, axis=1, mode="promise_in_bounds")
            found[k] = jnp.where(here, got, found[k])
    return found


def regrid(list_ref, offset, source, slot_ref, weight_ref, b):
    rows = slice(8 * b, 8 * b + 8)

    def row_of(k, r):
        at = offset + 8 * k + r
        return lambda: list_ref[at : at + 1, :]

    table = [[row_of(k, r) for r in range(8)] for k in range(COMP)]
    total = None
    for t in range(TERMS):
        slot = slot_ref[t, rows, :]
        found = lookup(table, slot >> 7, slot & (LANES - 1), 8 * source)
        found = [weight_ref[t, rows, :] * entry for entry in found]
        total = found if total is None else [a + b for a, b in zip(total, found)]
    return total


def fluxes(surface, sens_ref, weight, flux_ref):
    for k in range(COMP):
        total = sens_ref[k : k + 1, 0:1] * surface[0]
        for j in range(1, COMP):
            total = total + sens_ref[k : k + 1, j : j + 1] * surface[j]
        flux_ref[k] = weight * total


def pick(flux_ref, cell, out_ref, offset):
    def row_of(k, r):
        return lambda: flux_ref[k, r : r + 1, :]

    table = [[row_of(k, r) for r in range(ROWS)] for k in range(COMP)]
    found = lookup(table, cell >> 7, cell & (LANES - 1), 0)
    for k in range(COMP):
        out_ref[offset + 8 * k : offset + 8 * k + 8, :] = found[k]


def edges(upward, field_ref, dif_ref, vel_ref, out_ref):
    half = jnp.where(upward, -0.5, 0.5).astype(jnp.float32)
    last = jnp.where(upward, ROWS - 1, 0)
    column = jnp.broadcast_to(jnp.where(upward, LANES - 1, 0), (8, LANES))
    lane = lax.broadcasted_iota(jnp.int32, (8, LANES), 1)
    side = jnp.zeros((8, LANES), jnp.float32)
    for level in range(LEV):
        across = dif_ref[level] + half * vel_ref[0, level]
        along = dif_ref[level, pl.ds(last, 1), :] + half * vel_ref[1, level, pl.ds(last, 1), :]
        for k in range(COMP):
            at = LEV * k + level
            product = across * field_ref[k, level]
            for b in range(BLOCKS):
                edge = jnp.take_along_axis(product[8 * b : 8 * b + 8], column, axis=1, mode="promise_in_bounds")
                side = jnp.where(lane == PLANES * b + at, edge, side)
            out_ref[SIDE + at : SIDE + at + 1, :] = along * field_ref[k, level, pl.ds(last, 1), :]
    out_ref[LIST:SIDE, :] = side


def given(core, flux_ref, send_ref, give_ref):
    pick(flux_ref, send_ref[pl.ds(pl.multiple_of(16 * core, 8), 8), :], give_ref, 0)
    pick(flux_ref, send_ref[8:16, :], give_ref, KEEP)


def keep_kernel(field_ref, dif_ref, vel_ref, send_ref, flux_ref, keep_ref):
    core = lax.axis_index("sec")
    pick(flux_ref, send_ref[pl.ds(pl.multiple_of(16 - 16 * core, 8), 8), :], keep_ref, 0)
    edges(core == 0, field_ref, dif_ref, vel_ref, keep_ref)


def sea_weight(sea_ref, dist_ref):
    distance = dist_ref[...].astype(jnp.float32)
    blend = (distance + 1.0) / (distance + 9.0)
    return sea_ref[...].astype(jnp.float32) * blend


def start_kernel(
    sens_hbm, field_hbm, dif_hbm, vel_hbm, sea_hbm, dist_hbm, send_hbm,
    give_ref, flux_ref, sens_ref, field_ref, dif_ref, vel_ref, sea_ref, dist_ref, send_ref, sems,
):
    early = [(sens_hbm, sens_ref), (send_hbm, send_ref), (sea_hbm, sea_ref), (dist_hbm, dist_ref)]
    early += [(field_hbm.at[k, 0], field_ref.at[k, 0]) for k in range(COMP)]
    late = [(dif_hbm, dif_ref), (vel_hbm, vel_ref)]
    late += [(field_hbm.at[k, pl.ds(1, LEV - 1)], field_ref.at[k, pl.ds(1, LEV - 1)]) for k in range(COMP)]
    copies = [pltpu.make_async_copy(a, b, sems.at[i]) for i, (a, b) in enumerate(early + late)]
    for copy in copies:
        copy.start()
    for copy in copies[: len(early)]:
        copy.wait()

    core = lax.axis_index("sec")
    fluxes([field_ref[k, 0] for k in range(COMP)], sens_ref, sea_weight(sea_ref, dist_ref), flux_ref)
    given(core, flux_ref, send_ref, give_ref)
    for copy in copies[len(early) :]:
        copy.wait()
    edges(core != 0, field_ref, dif_ref, vel_ref, give_ref)


def inner_kernel(field_ref, dif_ref, vel_ref, slot_ref, weight_ref, near_ref, base_ref):
    lane = lax.broadcasted_iota(jnp.int32, (ROWS, LANES), 1)
    row = lax.broadcasted_iota(jnp.int32, (ROWS, LANES), 0)
    for level in range(LEV):
        dif = dif_ref[level]
        half_u = 0.5 * vel_ref[0, level]
        half_v = 0.5 * vel_ref[1, level]
        for k in range(COMP):
            plane = field_ref[k, level]
            east = jnp.where(lane == LANES - 1, 0.0, pltpu.roll((dif + half_u) * plane, LANES - 1, 1))
            west = jnp.where(lane == 0, 0.0, pltpu.roll((dif - half_u) * plane, 1, 1))
            north = jnp.where(row == ROWS - 1, 0.0, pltpu.roll((dif + half_v) * plane, ROWS - 1, 0))
            south = jnp.where(row == 0, 0.0, pltpu.roll((dif - half_v) * plane, 1, 0))
            base_ref[k, level] = plane - 4.0 * (dif * plane) + ((north + south) + (east + west))
    for b in range(BLOCKS):
        rows = slice(8 * b, 8 * b + 8)
        total = regrid(near_ref, KEEP, 1, slot_ref, weight_ref, b)
        for k in range(COMP):
            base_ref[k, 0, rows, :] = base_ref[k, 0, rows, :] + total[k]


def send_kernel(keep_ref, near_ref, lon_ref, lat_ref):
    lon_ref[:SIDE, :] = keep_ref[:SIDE, :]
    lon_ref[SIDE:, :] = near_ref[:SIDE, :]
    lat_ref[:PLANES, :] = keep_ref[SIDE:, :]
    lat_ref[PLANES : 2 * PLANES, :] = near_ref[SIDE:KEEP, :]


def turn_kernel(lon_ref, lat_ref, base_ref, back_ref, edge_ref):
    back_ref[:LIST, :] = lon_ref[:LIST, :]
    back_ref[LIST:SIDE, :] = lon_ref[SIDE + LIST :, :]
    back_ref[SIDE:, :] = lat_ref[PLANES : 2 * PLANES, :]
    edge_ref[:8, :] = lon_ref[LIST:SIDE, :]
    edge_ref[8:, :] = lat_ref[:PLANES, :]


def kept_kernel(slot_ref, weight_ref, lon_ref, part_ref):
    source = 2 * lax.axis_index("sec")
    for b in range(BLOCKS):
        total = regrid(lon_ref, SIDE, source, slot_ref, weight_ref, b)
        for k in range(COMP):
            part_ref[k, 8 * b : 8 * b + 8, :] = total[k]


def finish(core, base_ref, part_ref, slot_ref, weight_ref, edge_ref, back_ref, out_ref, ready):
    first = core == 0
    kept_side = edge_ref[:8, :]
    passed_side = back_ref[LIST:SIDE, :]
    from_west = jnp.where(first, kept_side, passed_side)
    from_east = jnp.where(first, passed_side, kept_side)
    lane = lax.broadcasted_iota(jnp.int32, (8, LANES), 1)
    row = lax.broadcasted_iota(jnp.int32, (8, LANES), 0)

    def completed(k, level, b):
        at = LEV * k + level
        j = PLANES * b + at
        edge_east = jnp.broadcast_to(from_east[:, j : j + 1], (8, LANES))
        edge_west = jnp.broadcast_to(from_west[:, j : j + 1], (8, LANES))
        edge = jnp.where(lane == LANES - 1, edge_east, jnp.where(lane == 0, edge_west, 0.0))
        if b == 0 or b == BLOCKS - 1:
            kept_row = edge_ref[8 + at : 9 + at, :]
            passed_row = back_ref[SIDE + at : SIDE + at + 1, :]
            pair = (kept_row, passed_row) if b == 0 else (passed_row, kept_row)
            end = jnp.broadcast_to(jnp.where(first, *pair), (8, LANES))
            edge = edge + jnp.where(row == (0 if b == 0 else 7), end, 0.0)
        return base_ref[k, level, 8 * b : 8 * b + 8, :] + edge

    for k in range(COMP):
        for level in range(1, LEV):
            for b in range(BLOCKS):
                out_ref[k, level, 8 * b : 8 * b + 8, :] = completed(k, level, b)
        ready(k)
    for b in range(BLOCKS):
        rows = slice(8 * b, 8 * b + 8)
        total = regrid(back_ref, 0, 2 - 2 * core, slot_ref, weight_ref, b)
        for k in range(COMP):
            out_ref[k, 0, rows, :] = completed(k, 0, b) + (part_ref[k, rows, :] + total[k])


def middle_kernel(
    sens_ref, base_ref, part_ref, slot_ref, weight_ref, edge_ref, back_ref, dif_ref, vel_ref, sea_ref, dist_ref, send_ref,
    out_ref, give_ref, flux_ref,
):
    core = lax.axis_index("sec")
    finish(core, base_ref, part_ref, slot_ref, weight_ref, edge_ref, back_ref, out_ref, lambda k: None)
    fluxes([out_ref[k, 0] for k in range(COMP)], sens_ref, sea_weight(sea_ref, dist_ref), flux_ref)
    given(core, flux_ref, send_ref, give_ref)
    edges(core != 0, out_ref, dif_ref, vel_ref, give_ref)


def last_kernel(base_ref, part_ref, slot_ref, weight_ref, edge_ref, back_ref, out_hbm, out_ref, sems):
    copies = [
        pltpu.make_async_copy(out_ref.at[k, pl.ds(1, LEV - 1)], out_hbm.at[k, pl.ds(1, LEV - 1)], sems.at[k]) for k in range(COMP)
    ]
    copies += [pltpu.make_async_copy(out_ref.at[k, 0], out_hbm.at[k, 0], sems.at[COMP + k]) for k in range(COMP)]
    finish(
        lax.axis_index("sec"), base_ref, part_ref, slot_ref, weight_ref, edge_ref, back_ref, out_ref, lambda k: copies[k].start()
    )
    for copy in copies[COMP:]:
        copy.start()
    for copy in copies:
        copy.wait()


def call(kernel, arrays, outs, scratch=(), space=pltpu.VMEM, out_space=pltpu.VMEM, cost=1 << 20):
    in_space = pl.BlockSpec(memory_space=space)
    to_space = pl.BlockSpec(memory_space=out_space)
    return pl.pallas_call(
        kernel,
        out_shape=[jax.ShapeDtypeStruct(shape, jnp.float32) for shape in outs],
        in_specs=[in_space] * len(arrays),
        out_specs=[to_space] * len(outs),
        scratch_shapes=list(scratch),
        compiler_params=pltpu.CompilerParams(vmem_limit_bytes=8 << 20),
        cost_estimate=pl.CostEstimate(flops=cost, transcendentals=0, bytes_accessed=cost),
    )(*arrays)


def routes(axis):
    count = lax.axis_size(axis)
    periodic = axis == "lon"
    pairs = []
    for i in range(count):
        if periodic or i + 1 < count:
            pairs.append((i, (i + 1) % count))
        if periodic or i > 0:
            pairs.append((count + i, count + (i - 1) % count))
    return pairs


def step(give, flux, field, dif, vel, send, take):
    near = lax.ppermute(give, "sec", [(0, 1), (1, 0)])
    (keep,) = call(keep_kernel, (field, dif, vel, send, flux), [(KEEP, LANES)])
    lon, lat = call(send_kernel, (keep, near), [(2 * SIDE, LANES), (2 * PLANES, LANES)])
    lon = lax.ppermute(lon, ("sec", "lon"), routes("lon"))
    lat = lax.ppermute(lat, ("sec", "lat"), routes("lat"))
    (base,) = call(inner_kernel, (field, dif, vel, *take, near), [field.shape])
    back, edge = call(turn_kernel, (lon, lat, base), [(KEEP, LANES), (8 + PLANES, LANES)])
    back = lax.ppermute(back, "sec", [(0, 1), (1, 0)])
    (part,) = call(kept_kernel, (*take, lon), [(COMP, ROWS, LANES)])
    return base, part, *take, edge, back


def on_device(
    adjoint,
    diffusivity,
    velocity,
    sensitivity,
    sea_mask,
    coast_distance,
    send_cells,
    recv_slots,
    regrid_weight,
):
    field = adjoint[0]
    sens = sensitivity[0]
    dif, vel = diffusivity[0], velocity[0]
    send = (sea_mask[0], coast_distance[0], send_cells.reshape(8 * PEERS, LANES))
    take = (recv_slots[0], regrid_weight[0])
    messages = [(GIVE, LANES), (COMP, ROWS, LANES)]
    fresh = (sens, field, dif, vel, *send)
    held = [pltpu.VMEM(a.shape, a.dtype) for a in fresh]
    fresh = [pltpu.with_memory_space_constraint(a, pltpu.HBM) for a in fresh]
    sems = pltpu.SemaphoreType.DMA((6 + 2 * COMP,))
    give, flux = call(start_kernel, fresh, messages, [*held, sems], pltpu.HBM)
    state = step(give, flux, field, dif, vel, send[2], take)
    field, give, flux = call(middle_kernel, (sens, *state, dif, vel, *send), [field.shape] + messages)
    state = step(give, flux, field, dif, vel, send[2], take)
    scratch = [pltpu.VMEM(field.shape, jnp.float32), pltpu.SemaphoreType.DMA((2 * COMP,))]
    (field,) = call(last_kernel, state, [field.shape], scratch, out_space=pltpu.HBM)
    return field[None]


def solution(mesh):
    placed = (
        P("sec", None, None, "lat", "lon"),
        P("sec", None, "lat", "lon"),
        P("sec", None, None, "lat", "lon"),
        P("sec", None, None),
        P("sec", "lat", "lon"),
        P("sec", "lat", "lon"),
        P("sec", "lat", "lon", None),
        P("sec", None, "lat", "lon"),
        P("sec", None, "lat", "lon"),
    )
    return jax.shard_map(
        on_device,
        mesh=mesh,
        in_specs=placed,
        out_specs=P("sec", None, None, "lat", "lon"),
        check_vma=False,
    )
```

```python
import jax
import jax.numpy as jnp
from jax import lax
from jax.experimental import pallas as pl
from jax.experimental.pallas import tpu as pltpu
from jax.sharding import PartitionSpec as P

COMP = 4
LEV = 4
TERMS = 4
ROWS = 32
LANES = 128
BLOCKS = ROWS // 8
PEERS = 3
PLANES = COMP * LEV

LIST = 8 * COMP
SIDE = LIST + 8
KEEP = SIDE + PLANES
GIVE = KEEP + LIST
SURFACE = GIVE
COEF = SURFACE + COMP * ROWS
SEA = COEF + 3 * ROWS
SLOT = SEA + ROWS
WEIGHT = SLOT + TERMS * ROWS
CELL = WEIGHT + TERMS * ROWS
SENS = CELL + 8 * PEERS
FIRST = SENS + 8
STRIP = 2 * SIDE + 2 * PLANES
BACK = STRIP + 2 * (8 + PLANES)


def lookup(rows, high, low, first_row):
    found = [jnp.zeros((8, LANES), jnp.float32) for _ in range(COMP)]
    for r in range(len(rows[0])):
        here = high == first_row + r
        for k in range(COMP):
            row = jnp.broadcast_to(rows[k][r](), (8, LANES))
            got = jnp.take_along_axis(row, low, axis=1, mode="promise_in_bounds")
            found[k] = jnp.where(here, got, found[k])
    return found


def regrid(list_ref, offset, source, entries, b):
    slots, weights = entries

    def row_of(k, r):
        at = offset + 8 * k + r
        return lambda: list_ref[at : at + 1, :]

    table = [[row_of(k, r) for r in range(8)] for k in range(COMP)]
    total = None
    for t in range(TERMS):
        slot = slots(t, b)
        found = lookup(table, slot >> 7, slot & (LANES - 1), 8 * source)
        found = [weights(t, b) * entry for entry in found]
        total = found if total is None else [a + b for a, b in zip(total, found)]
    return total


def own_entries(slot_ref, weight_ref):
    return (lambda t, b: slot_ref[t, 8 * b : 8 * b + 8, :]), (lambda t, b: weight_ref[t, 8 * b : 8 * b + 8, :])


def near_entries(near_ref):
    def rows(base, t, b):
        return near_ref[base + ROWS * t + 8 * b : base + ROWS * t + 8 * b + 8, :]

    return (lambda t, b: rows(SLOT, t, b).astype(jnp.int32)), (lambda t, b: rows(WEIGHT, t, b))


def fluxes(surface, sens_ref, weight, flux_ref):
    for k in range(COMP):
        total = sens_ref[k : k + 1, 0:1] * surface[0]
        for j in range(1, COMP):
            total = total + sens_ref[k : k + 1, j : j + 1] * surface[j]
        flux_ref[k] = weight * total


def pick(flux_ref, cell, out_ref, offset):
    def row_of(k, r):
        return lambda: flux_ref[k, r : r + 1, :]

    table = [[row_of(k, r) for r in range(ROWS)] for k in range(COMP)]
    found = lookup(table, cell >> 7, cell & (LANES - 1), 0)
    for k in range(COMP):
        out_ref[offset + 8 * k : offset + 8 * k + 8, :] = found[k]


def direction(upward):
    half = jnp.where(upward, -0.5, 0.5).astype(jnp.float32)
    last = jnp.where(upward, ROWS - 1, 0)
    column = jnp.broadcast_to(jnp.where(upward, LANES - 1, 0), (8, LANES))
    return half, last, column


def pull(value, index):
    return jnp.take_along_axis(value, index, axis=1, mode="promise_in_bounds")


def edges(upward, field_ref, dif_ref, vel_ref, side_ref, side_at, row_ref, row_at):
    half, last, column = direction(upward)
    lane = lax.broadcasted_iota(jnp.int32, (8, LANES), 1)
    side = jnp.zeros((8, LANES), jnp.float32)
    for level in range(LEV):
        across = dif_ref[level] + half * vel_ref[0, level]
        along = dif_ref[level, pl.ds(last, 1), :] + half * vel_ref[1, level, pl.ds(last, 1), :]
        for k in range(COMP):
            at = LEV * k + level
            product = across * field_ref[k, level]
            for b in range(BLOCKS):
                side = jnp.where(lane == PLANES * b + at, pull(product[8 * b : 8 * b + 8], column), side)
            row_ref[row_at + at : row_at + at + 1, :] = along * field_ref[k, level, pl.ds(last, 1), :]
    side_ref[side_at : side_at + 8, :] = side


def given(core, flux_ref, send_ref, give_ref):
    pick(flux_ref, send_ref[pl.ds(pl.multiple_of(16 * core, 8), 8), :], give_ref, 0)
    pick(flux_ref, send_ref[8:16, :], give_ref, KEEP)


def keep_kernel(field_ref, dif_ref, vel_ref, send_ref, flux_ref, keep_ref):
    core = lax.axis_index("sec")
    pick(flux_ref, send_ref[pl.ds(pl.multiple_of(16 - 16 * core, 8), 8), :], keep_ref, 0)
    edges(core == 0, field_ref, dif_ref, vel_ref, keep_ref, LIST, keep_ref, SIDE)


def sea_weight(sea_ref, dist_ref):
    distance = dist_ref[...].astype(jnp.float32)
    blend = (distance + 1.0) / (distance + 9.0)
    return sea_ref[...].astype(jnp.float32) * blend


def start_kernel(
    sens_hbm, field_hbm, dif_hbm, vel_hbm, sea_hbm, dist_hbm, send_hbm, slot_hbm, weight_hbm,
    give_ref, flux_ref, sens_ref, field_ref, dif_ref, vel_ref, sea_ref, dist_ref, send_ref, slot_ref, weight_ref, sems,
):
    early = [(sens_hbm, sens_ref), (send_hbm, send_ref), (sea_hbm, sea_ref), (dist_hbm, dist_ref)]
    early += [(field_hbm.at[:, 0], field_ref.at[:, 0])]
    late = [(dif_hbm, dif_ref), (vel_hbm, vel_ref), (slot_hbm, slot_ref), (weight_hbm, weight_ref)]
    late += [(field_hbm.at[:, pl.ds(1, LEV - 1)], field_ref.at[:, pl.ds(1, LEV - 1)])]
    copies = [pltpu.make_async_copy(a, b, sems.at[i]) for i, (a, b) in enumerate(early + late)]
    for copy in copies:
        copy.start()
    for copy in copies[: len(early)]:
        copy.wait()

    core = lax.axis_index("sec")
    sea = sea_weight(sea_ref, dist_ref)
    fluxes([field_ref[k, 0] for k in range(COMP)], sens_ref, sea, flux_ref)
    given(core, flux_ref, send_ref, give_ref)
    give_ref[SEA:SLOT, :] = sea
    give_ref[CELL:SENS, :] = send_ref[...].astype(jnp.float32)
    give_ref[SENS:, :] = jnp.zeros((8, LANES), jnp.float32)
    give_ref[SENS : SENS + COMP, 0:COMP] = sens_ref[...]
    for copy in copies[len(early) :]:
        copy.wait()
    edges(core != 0, field_ref, dif_ref, vel_ref, give_ref, LIST, give_ref, SIDE)
    for k in range(COMP):
        give_ref[SURFACE + ROWS * k : SURFACE + ROWS * k + ROWS, :] = field_ref[k, 0]
    for i, plane in enumerate((dif_ref[0], vel_ref[0, 0], vel_ref[1, 0])):
        give_ref[COEF + ROWS * i : COEF + ROWS * i + ROWS, :] = plane
    for t in range(TERMS):
        give_ref[SLOT + ROWS * t : SLOT + ROWS * t + ROWS, :] = slot_ref[t].astype(jnp.float32)
        give_ref[WEIGHT + ROWS * t : WEIGHT + ROWS * t + ROWS, :] = weight_ref[t]


def inside(plane, dif, half_u, half_v):
    lane = lax.broadcasted_iota(jnp.int32, (ROWS, LANES), 1)
    row = lax.broadcasted_iota(jnp.int32, (ROWS, LANES), 0)
    east = jnp.where(lane == LANES - 1, 0.0, pltpu.roll((dif + half_u) * plane, LANES - 1, 1))
    west = jnp.where(lane == 0, 0.0, pltpu.roll((dif - half_u) * plane, 1, 1))
    north = jnp.where(row == ROWS - 1, 0.0, pltpu.roll((dif + half_v) * plane, ROWS - 1, 0))
    south = jnp.where(row == 0, 0.0, pltpu.roll((dif - half_v) * plane, 1, 0))
    return plane - 4.0 * (dif * plane) + ((north + south) + (east + west))


def inner(field_ref, dif_ref, vel_ref, entries, list_ref, offset, base_ref):
    for level in range(LEV):
        for k in range(COMP):
            base_ref[k, level] = inside(field_ref[k, level], dif_ref[level], 0.5 * vel_ref[0, level], 0.5 * vel_ref[1, level])
    for b in range(BLOCKS):
        rows = slice(8 * b, 8 * b + 8)
        total = regrid(list_ref, offset, 1, entries, b)
        for k in range(COMP):
            base_ref[k, 0, rows, :] = base_ref[k, 0, rows, :] + total[k]


def first_inner_kernel(field_ref, dif_ref, vel_ref, slot_ref, weight_ref, near_ref, give_ref, base_ref, other_ref, strip_ref):
    inner(field_ref, dif_ref, vel_ref, own_entries(slot_ref, weight_ref), near_ref, KEEP, base_ref)
    dif = near_ref[COEF : COEF + ROWS, :]
    half_u = 0.5 * near_ref[COEF + ROWS : COEF + 2 * ROWS, :]
    half_v = 0.5 * near_ref[COEF + 2 * ROWS : COEF + 3 * ROWS, :]
    for k in range(COMP):
        other_ref[k] = inside(near_ref[SURFACE + ROWS * k : SURFACE + ROWS * k + ROWS, :], dif, half_u, half_v)
    for b in range(BLOCKS):
        rows = slice(8 * b, 8 * b + 8)
        total = regrid(give_ref, KEEP, 1, near_entries(near_ref), b)
        for k in range(COMP):
            other_ref[k, rows, :] = other_ref[k, rows, :] + total[k]

    half, last, column = direction(lax.axis_index("sec") != 0)
    lane = lax.broadcasted_iota(jnp.int32, (8, LANES), 1)
    side = jnp.zeros((8, LANES), jnp.float32)
    factor = jnp.zeros((8, LANES), jnp.float32)
    strip_ref[8 : 8 + PLANES, :] = jnp.zeros((PLANES, LANES), jnp.float32)
    strip_ref[16 + PLANES :, :] = jnp.zeros((PLANES, LANES), jnp.float32)
    for level in range(1, LEV):
        across = dif_ref[level] + half * vel_ref[0, level]
        along = dif_ref[level, pl.ds(last, 1), :] + half * vel_ref[1, level, pl.ds(last, 1), :]
        for b in range(BLOCKS):
            here = ((lane >> 4) == b) & ((lane & (LEV - 1)) == level)
            factor = jnp.where(here, pull(across[8 * b : 8 * b + 8], column), factor)
        for k in range(COMP):
            at = LEV * k + level
            for b in range(BLOCKS):
                side = jnp.where(lane == PLANES * b + at, pull(base_ref[k, level, 8 * b : 8 * b + 8, :], column), side)
            strip_ref[8 + at : 9 + at, :] = base_ref[k, level, pl.ds(last, 1), :]
            strip_ref[16 + PLANES + at : 17 + PLANES + at, :] = along
    strip_ref[:8, :] = side
    strip_ref[8 + PLANES : 16 + PLANES, :] = factor


def second_inner_kernel(field_ref, dif_ref, vel_ref, slot_ref, weight_ref, near_ref, flux_ref, base_ref, list_ref):
    pick(flux_ref, near_ref[CELL + 8 : CELL + 16, :].astype(jnp.int32), list_ref, 0)
    inner(field_ref, dif_ref, vel_ref, own_entries(slot_ref, weight_ref), list_ref, 0, base_ref)


def send_kernel(keep_ref, near_ref, lon_ref, lat_ref):
    lon_ref[:SIDE, :] = keep_ref[:SIDE, :]
    lon_ref[SIDE:, :] = near_ref[:SIDE, :]
    lat_ref[:PLANES, :] = keep_ref[SIDE:, :]
    lat_ref[PLANES : 2 * PLANES, :] = near_ref[SIDE:KEEP, :]


def first_turn_kernel(lon_ref, lat_ref, strip_ref, back_ref):
    back_ref[: 2 * SIDE, :] = lon_ref[...]
    back_ref[2 * SIDE : STRIP, :] = lat_ref[...]
    back_ref[STRIP:, :] = strip_ref[...]


def second_turn_kernel(lon_ref, lat_ref, base_ref, back_ref, edge_ref):
    back_ref[:LIST, :] = lon_ref[:LIST, :]
    back_ref[LIST:SIDE, :] = lon_ref[SIDE + LIST :, :]
    back_ref[SIDE:, :] = lat_ref[PLANES : 2 * PLANES, :]
    edge_ref[:8, :] = lon_ref[LIST:SIDE, :]
    edge_ref[8:, :] = lat_ref[:PLANES, :]


def kept(list_ref, offset, entries, part_ref):
    source = 2 * lax.axis_index("sec")
    for b in range(BLOCKS):
        total = regrid(list_ref, offset, source, entries, b)
        for k in range(COMP):
            part_ref[k, 8 * b : 8 * b + 8, :] = total[k]


def first_kept_kernel(slot_ref, weight_ref, near_ref, lon_ref, part_ref, other_part_ref):
    kept(lon_ref, SIDE, own_entries(slot_ref, weight_ref), part_ref)
    kept(lon_ref, 0, near_entries(near_ref), other_part_ref)


def second_kept_kernel(slot_ref, weight_ref, lon_ref, part_ref):
    kept(lon_ref, SIDE, own_entries(slot_ref, weight_ref), part_ref)


def around(core, kept_side, passed_side, kept_row, passed_row):
    first = core == 0
    from_west = jnp.where(first, kept_side, passed_side)
    from_east = jnp.where(first, passed_side, kept_side)
    lane = lax.broadcasted_iota(jnp.int32, (8, LANES), 1)
    row = lax.broadcasted_iota(jnp.int32, (8, LANES), 0)

    def arrived(k, level, b):
        at = LEV * k + level
        j = PLANES * b + at
        edge_east = jnp.broadcast_to(from_east[:, j : j + 1], (8, LANES))
        edge_west = jnp.broadcast_to(from_west[:, j : j + 1], (8, LANES))
        edge = jnp.where(lane == LANES - 1, edge_east, jnp.where(lane == 0, edge_west, 0.0))
        if b == 0 or b == BLOCKS - 1:
            pair = (kept_row(at), passed_row(at)) if b == 0 else (passed_row(at), kept_row(at))
            end = jnp.broadcast_to(jnp.where(first, *pair), (8, LANES))
            edge = edge + jnp.where(row == (0 if b == 0 else 7), end, 0.0)
        return edge

    return arrived


def finish(core, base_ref, part_ref, entries, arrived, list_ref, out_ref, ready):
    for k in range(COMP):
        for level in range(1, LEV):
            for b in range(BLOCKS):
                rows = slice(8 * b, 8 * b + 8)
                out_ref[k, level, rows, :] = base_ref[k, level, rows, :] + arrived(k, level, b)
    ready()
    for b in range(BLOCKS):
        rows = slice(8 * b, 8 * b + 8)
        total = regrid(list_ref, 0, 2 - 2 * core, entries, b)
        for k in range(COMP):
            out_ref[k, 0, rows, :] = (base_ref[k, 0, rows, :] + arrived(k, 0, b)) + (part_ref[k, rows, :] + total[k])


def other_edges(core, surface_ref, near_ref, lat_ref, lon_ref, back_ref, out_lon_ref, out_lat_ref):
    first = core == 0
    half, last, column = direction(first)
    lane = lax.broadcasted_iota(jnp.int32, (8, LANES), 1)
    row = lax.broadcasted_iota(jnp.int32, (8, LANES), 0)
    passed_side = back_ref[LIST:SIDE, :]
    kept_side = lon_ref[SIDE + LIST :, :]
    from_west = jnp.where(first, kept_side, passed_side)
    from_east = jnp.where(first, passed_side, kept_side)

    corner_north = jnp.zeros((8, LANES), jnp.float32)
    corner_south = jnp.zeros((8, LANES), jnp.float32)
    for i in range(PLANES // 8):
        passed = back_ref[2 * SIDE + 8 * i : 2 * SIDE + 8 * i + 8, :]
        kept_rows = lat_ref[PLANES + 8 * i : PLANES + 8 * i + 8, :]
        south = pull(jnp.where(first, kept_rows, passed), column)
        north = pull(jnp.where(first, passed, kept_rows), column)
        corner_south = corner_south + jnp.where(lane == row + 8 * i, south, 0.0)
        corner_north = corner_north + jnp.where(lane == row + 8 * i + PLANES * (BLOCKS - 1), north, 0.0)
        index = row + 8 * i + jnp.where(first, PLANES * (BLOCKS - 1), 0)
        end_west = jnp.where(first, from_west[7:8], from_west[0:1])
        end_east = jnp.where(first, from_east[7:8], from_east[0:1])
        west = pull(jnp.broadcast_to(end_west, (8, LANES)), index)
        east = pull(jnp.broadcast_to(end_east, (8, LANES)), index)
        ends = jnp.where(lane == LANES - 1, east, jnp.where(lane == 0, west, 0.0))
        at = STRIP + 8 + 8 * i
        line = back_ref[at : at + 8, :] + passed + ends
        factor = back_ref[at + 8 + PLANES : at + 16 + PLANES, :]
        out_lat_ref[PLANES + 8 * i : PLANES + 8 * i + 8, :] = factor * line
    corner_south = jnp.broadcast_to(jnp.sum(corner_south, axis=0, keepdims=True), (8, LANES))
    corner_north = jnp.broadcast_to(jnp.sum(corner_north, axis=0, keepdims=True), (8, LANES))
    corner = jnp.where(row == 0, corner_south, jnp.where(row == 7, corner_north, 0.0))
    factor = back_ref[STRIP + 8 + PLANES : STRIP + 16 + PLANES, :]
    side = factor * (back_ref[STRIP : STRIP + 8, :] + passed_side + corner)

    across = near_ref[COEF : COEF + ROWS, :] + half * near_ref[COEF + ROWS : COEF + 2 * ROWS, :]
    along = near_ref[pl.ds(COEF + last, 1), :] + half * near_ref[pl.ds(COEF + 2 * ROWS + last, 1), :]
    for k in range(COMP):
        at = LEV * k
        product = across * surface_ref[k]
        for b in range(BLOCKS):
            side = jnp.where(lane == PLANES * b + at, pull(product[8 * b : 8 * b + 8], column), side)
        out_lat_ref[PLANES + at : PLANES + at + 1, :] = along * surface_ref[k, pl.ds(last, 1), :]
    out_lon_ref[SIDE + LIST :, :] = side


def middle_kernel(
    sens_ref, base_ref, part_ref, other_base_ref, other_part_ref, slot_ref, weight_ref, near_ref, lon_ref, lat_ref, back_ref,
    dif_ref, vel_ref, sea_ref, dist_ref, send_ref,
    out_ref, out_lon_ref, out_lat_ref, other_flux_ref, flux_ref, surface_ref,
):
    core = lax.axis_index("sec")
    arrived = around(
        core, lon_ref[LIST:SIDE, :], back_ref[SIDE + LIST : 2 * SIDE, :],
        lambda at: lat_ref[at : at + 1, :], lambda at: back_ref[2 * SIDE + PLANES + at : 2 * SIDE + PLANES + at + 1, :],
    )
    finish(core, base_ref, part_ref, own_entries(slot_ref, weight_ref), arrived, back_ref, out_ref, lambda: None)
    arrived = around(
        core, lon_ref[SIDE + LIST :, :], back_ref[LIST:SIDE, :],
        lambda at: lat_ref[PLANES + at : PLANES + at + 1, :], lambda at: back_ref[2 * SIDE + at : 2 * SIDE + at + 1, :],
    )
    for b in range(BLOCKS):
        rows = slice(8 * b, 8 * b + 8)
        total = regrid(back_ref, SIDE, 2 - 2 * core, near_entries(near_ref), b)
        for k in range(COMP):
            surface_ref[k, rows, :] = (other_base_ref[k, rows, :] + arrived(k, 0, b)) + (other_part_ref[k, rows, :] + total[k])
    fluxes([out_ref[k, 0] for k in range(COMP)], sens_ref, sea_weight(sea_ref, dist_ref), flux_ref)
    other_sens = near_ref[SENS : SENS + COMP, :]
    fluxes([surface_ref[k] for k in range(COMP)], other_sens, near_ref[SEA:SLOT, :], other_flux_ref)
    pick(flux_ref, send_ref[pl.ds(pl.multiple_of(16 - 16 * core, 8), 8), :], out_lon_ref, 0)
    cell = near_ref[pl.ds(pl.multiple_of(CELL + 16 - 16 * core, 8), 8), :].astype(jnp.int32)
    pick(other_flux_ref, cell, out_lon_ref, SIDE)
    edges(core == 0, out_ref, dif_ref, vel_ref, out_lon_ref, LIST, out_lat_ref, 0)
    other_edges(core, surface_ref, near_ref, lat_ref, lon_ref, back_ref, out_lon_ref, out_lat_ref)


def last_kernel(base_ref, part_ref, slot_ref, weight_ref, edge_ref, back_ref, out_hbm, out_ref, sems):
    core = lax.axis_index("sec")
    deep = pltpu.make_async_copy(out_ref.at[:, pl.ds(1, LEV - 1)], out_hbm.at[:, pl.ds(1, LEV - 1)], sems.at[0])
    top = pltpu.make_async_copy(out_ref.at[:, 0], out_hbm.at[:, 0], sems.at[1])
    arrived = around(
        core, edge_ref[:8, :], back_ref[LIST:SIDE, :],
        lambda at: edge_ref[8 + at : 9 + at, :], lambda at: back_ref[SIDE + at : SIDE + at + 1, :],
    )
    finish(core, base_ref, part_ref, own_entries(slot_ref, weight_ref), arrived, back_ref, out_ref, deep.start)
    top.start()
    deep.wait()
    top.wait()


def call(kernel, arrays, outs, scratch=(), space=pltpu.VMEM, out_space=pltpu.VMEM, cost=1 << 20):
    in_space = pl.BlockSpec(memory_space=space)
    to_space = pl.BlockSpec(memory_space=out_space)
    return pl.pallas_call(
        kernel,
        out_shape=[jax.ShapeDtypeStruct(shape, jnp.float32) for shape in outs],
        in_specs=[in_space] * len(arrays),
        out_specs=[to_space] * len(outs),
        scratch_shapes=list(scratch),
        compiler_params=pltpu.CompilerParams(vmem_limit_bytes=8 << 20),
        cost_estimate=pl.CostEstimate(flops=cost, transcendentals=0, bytes_accessed=cost),
    )(*arrays)


def routes(axis):
    count = lax.axis_size(axis)
    periodic = axis == "lon"
    pairs = []
    for i in range(count):
        if periodic or i + 1 < count:
            pairs.append((i, (i + 1) % count))
        if periodic or i > 0:
            pairs.append((count + i, count + (i - 1) % count))
    return pairs


def on_device(
    adjoint,
    diffusivity,
    velocity,
    sensitivity,
    sea_mask,
    coast_distance,
    send_cells,
    recv_slots,
    regrid_weight,
):
    field = adjoint[0]
    sens = sensitivity[0]
    dif, vel = diffusivity[0], velocity[0]
    send = (sea_mask[0], coast_distance[0], send_cells.reshape(8 * PEERS, LANES))
    take = (recv_slots[0], regrid_weight[0])
    swap = [(0, 1), (1, 0)]
    surface = (COMP, ROWS, LANES)
    lon_rows, lat_rows = (2 * SIDE, LANES), (2 * PLANES, LANES)
    fresh = (sens, field, dif, vel, *send, *take)
    held = [pltpu.VMEM(a.shape, a.dtype) for a in fresh]
    fresh = [pltpu.with_memory_space_constraint(a, pltpu.HBM) for a in fresh]
    sems = pltpu.SemaphoreType.DMA((10,))
    give, flux = call(start_kernel, fresh, [(FIRST, LANES), surface], [*held, sems], pltpu.HBM)

    near = lax.ppermute(give, "sec", swap)
    (keep,) = call(keep_kernel, (field, dif, vel, send[2], flux), [(KEEP, LANES)])
    lon, lat = call(send_kernel, (keep, near), [lon_rows, lat_rows])
    lon = lax.ppermute(lon, ("sec", "lon"), routes("lon"))
    lat = lax.ppermute(lat, ("sec", "lat"), routes("lat"))
    base, other_base, strip = call(
        first_inner_kernel, (field, dif, vel, *take, near, give), [field.shape, surface, (BACK - STRIP, LANES)]
    )
    (back,) = call(first_turn_kernel, (lon, lat, strip), [(BACK, LANES)])
    back = lax.ppermute(back, "sec", swap)
    part, other_part = call(first_kept_kernel, (*take, near, lon), [surface, surface])

    scratch = [pltpu.VMEM(surface, jnp.float32)] * 2
    field, lon, lat, flux = call(
        middle_kernel,
        (sens, base, part, other_base, other_part, *take, near, lon, lat, back, dif, vel, *send),
        [field.shape, lon_rows, lat_rows, surface],
        scratch,
    )
    lon = lax.ppermute(lon, ("sec", "lon"), routes("lon"))
    lat = lax.ppermute(lat, ("sec", "lat"), routes("lat"))
    scratch = [pltpu.VMEM((LIST, LANES), jnp.float32)]
    (base,) = call(second_inner_kernel, (field, dif, vel, *take, near, flux), [field.shape], scratch)
    back, edge = call(second_turn_kernel, (lon, lat, base), [(KEEP, LANES), (8 + PLANES, LANES)])
    back = lax.ppermute(back, "sec", swap)
    (part,) = call(second_kept_kernel, (*take, lon), [surface])
    scratch = [pltpu.VMEM(field.shape, jnp.float32), pltpu.SemaphoreType.DMA((2,))]
    (field,) = call(last_kernel, (base, part, *take, edge, back), [field.shape], scratch, out_space=pltpu.HBM)
    return field[None]


def solution(mesh):
    placed = (
        P("sec", None, None, "lat", "lon"),
        P("sec", None, "lat", "lon"),
        P("sec", None, None, "lat", "lon"),
        P("sec", None, None),
        P("sec", "lat", "lon"),
        P("sec", "lat", "lon"),
        P("sec", "lat", "lon", None),
        P("sec", None, "lat", "lon"),
        P("sec", None, "lat", "lon"),
    )
    return jax.shard_map(
        on_device,
        mesh=mesh,
        in_specs=placed,
        out_specs=P("sec", None, None, "lat", "lon"),
        check_vma=False,
    )
```

```python
import jax
import jax.numpy as jnp
from jax import lax
from jax.experimental import pallas as pl
from jax.experimental.pallas import tpu as pltpu
from jax.sharding import PartitionSpec as P

COMP = 4
LEV = 4
TERMS = 4
ROWS = 32
LANES = 128
BLOCKS = ROWS // 8
PEERS = 3
PLANES = COMP * LEV

LIST = 8 * COMP
SIDE = LIST + 8
KEEP = SIDE + PLANES
GIVE = KEEP + LIST
SURFACE = GIVE
COEF = SURFACE + COMP * ROWS
SEA = COEF + 3 * ROWS
SLOT = SEA + ROWS
WEIGHT = SLOT + TERMS * ROWS
CELL = WEIGHT + TERMS * ROWS
SENS = CELL + 8 * PEERS
FIRST = SENS + 8
STRIP = 2 * SIDE + 2 * PLANES
BACK = STRIP + 2 * (8 + PLANES)


def lookup(rows, high, low, first_row):
    found = [jnp.zeros((8, LANES), jnp.float32) for _ in range(COMP)]
    for r in range(len(rows[0])):
        here = high == first_row + r
        for k in range(COMP):
            row = jnp.broadcast_to(rows[k][r](), (8, LANES))
            got = jnp.take_along_axis(row, low, axis=1, mode="promise_in_bounds")
            found[k] = jnp.where(here, got, found[k])
    return found


def regrid(list_ref, offset, source, entries, b):
    slots, weights = entries

    def row_of(k, r):
        at = offset + 8 * k + r
        return lambda: list_ref[at : at + 1, :]

    table = [[row_of(k, r) for r in range(8)] for k in range(COMP)]
    total = None
    for t in range(TERMS):
        slot = slots(t, b)
        found = lookup(table, slot >> 7, slot & (LANES - 1), 8 * source)
        found = [weights(t, b) * entry for entry in found]
        total = found if total is None else [a + b for a, b in zip(total, found)]
    return total


def entries_of(message_ref):
    def rows(base, t, b):
        return message_ref[base + ROWS * t + 8 * b : base + ROWS * t + 8 * b + 8, :]

    return (lambda t, b: rows(SLOT, t, b).astype(jnp.int32)), (lambda t, b: rows(WEIGHT, t, b))


def fluxes(surface, sens_ref, weight, flux_ref):
    for k in range(COMP):
        total = sens_ref[k : k + 1, 0:1] * surface[0]
        for j in range(1, COMP):
            total = total + sens_ref[k : k + 1, j : j + 1] * surface[j]
        flux_ref[k] = weight * total


def pick(flux_ref, cell, out_ref, offset):
    def row_of(k, r):
        return lambda: flux_ref[k, r : r + 1, :]

    table = [[row_of(k, r) for r in range(ROWS)] for k in range(COMP)]
    found = lookup(table, cell >> 7, cell & (LANES - 1), 0)
    for k in range(COMP):
        out_ref[offset + 8 * k : offset + 8 * k + 8, :] = found[k]


def direction(upward):
    half = jnp.where(upward, -0.5, 0.5).astype(jnp.float32)
    last = jnp.where(upward, ROWS - 1, 0)
    column = jnp.broadcast_to(jnp.where(upward, LANES - 1, 0), (8, LANES))
    return half, last, column


def pull(value, index):
    return jnp.take_along_axis(value, index, axis=1, mode="promise_in_bounds")


def edges(upward, field_ref, dif_ref, vel_ref, side_ref, side_at, row_ref, row_at):
    half, last, column = direction(upward)
    lane = lax.broadcasted_iota(jnp.int32, (8, LANES), 1)
    side = jnp.zeros((8, LANES), jnp.float32)
    for level in range(LEV):
        across = dif_ref[level] + half * vel_ref[0, level]
        along = dif_ref[level, pl.ds(last, 1), :] + half * vel_ref[1, level, pl.ds(last, 1), :]
        for k in range(COMP):
            at = LEV * k + level
            product = across * field_ref[k, level]
            for b in range(BLOCKS):
                side = jnp.where(lane == PLANES * b + at, pull(product[8 * b : 8 * b + 8], column), side)
            row_ref[row_at + at : row_at + at + 1, :] = along * field_ref[k, level, pl.ds(last, 1), :]
    side_ref[side_at : side_at + 8, :] = side


def given(core, flux_ref, send_ref, give_ref):
    pick(flux_ref, send_ref[pl.ds(pl.multiple_of(16 * core, 8), 8), :], give_ref, 0)
    pick(flux_ref, send_ref[8:16, :], give_ref, KEEP)


def sea_weight(sea_ref, dist_ref):
    distance = dist_ref[...].astype(jnp.float32)
    blend = (distance + 1.0) / (distance + 9.0)
    return sea_ref[...].astype(jnp.float32) * blend


def start_kernel(
    sens_hbm, field_hbm, dif_hbm, vel_hbm, sea_hbm, dist_hbm, send_hbm, slot_hbm, weight_hbm,
    give_ref, flux_ref, sens_ref, field_ref, dif_ref, vel_ref, sea_ref, dist_ref, send_ref, slot_ref, weight_ref, sems,
):
    early = [(sens_hbm, sens_ref), (send_hbm, send_ref), (sea_hbm, sea_ref), (dist_hbm, dist_ref)]
    early += [(field_hbm.at[:, 0], field_ref.at[:, 0])]
    late = [(dif_hbm, dif_ref), (vel_hbm, vel_ref), (slot_hbm, slot_ref), (weight_hbm, weight_ref)]
    late += [(field_hbm.at[:, pl.ds(1, LEV - 1)], field_ref.at[:, pl.ds(1, LEV - 1)])]
    copies = [pltpu.make_async_copy(a, b, sems.at[i]) for i, (a, b) in enumerate(early + late)]
    for copy in copies:
        copy.start()
    for copy in copies[: len(early)]:
        copy.wait()

    core = lax.axis_index("sec")
    sea = sea_weight(sea_ref, dist_ref)
    fluxes([field_ref[k, 0] for k in range(COMP)], sens_ref, sea, flux_ref)
    given(core, flux_ref, send_ref, give_ref)
    give_ref[SEA:SLOT, :] = sea
    give_ref[CELL:SENS, :] = send_ref[...].astype(jnp.float32)
    give_ref[SENS:, :] = jnp.zeros((8, LANES), jnp.float32)
    give_ref[SENS : SENS + COMP, 0:COMP] = sens_ref[...]
    for copy in copies[len(early) :]:
        copy.wait()
    edges(core != 0, field_ref, dif_ref, vel_ref, give_ref, LIST, give_ref, SIDE)
    for k in range(COMP):
        give_ref[SURFACE + ROWS * k : SURFACE + ROWS * k + ROWS, :] = field_ref[k, 0]
    for i, plane in enumerate((dif_ref[0], vel_ref[0, 0], vel_ref[1, 0])):
        give_ref[COEF + ROWS * i : COEF + ROWS * i + ROWS, :] = plane
    for t in range(TERMS):
        give_ref[SLOT + ROWS * t : SLOT + ROWS * t + ROWS, :] = slot_ref[t].astype(jnp.float32)
        give_ref[WEIGHT + ROWS * t : WEIGHT + ROWS * t + ROWS, :] = weight_ref[t]


def inside(plane, dif, half_u, half_v):
    lane = lax.broadcasted_iota(jnp.int32, (ROWS, LANES), 1)
    row = lax.broadcasted_iota(jnp.int32, (ROWS, LANES), 0)
    east = jnp.where(lane == LANES - 1, 0.0, pltpu.roll((dif + half_u) * plane, LANES - 1, 1))
    west = jnp.where(lane == 0, 0.0, pltpu.roll((dif - half_u) * plane, 1, 1))
    north = jnp.where(row == ROWS - 1, 0.0, pltpu.roll((dif + half_v) * plane, ROWS - 1, 0))
    south = jnp.where(row == 0, 0.0, pltpu.roll((dif - half_v) * plane, 1, 0))
    return plane - 4.0 * (dif * plane) + ((north + south) + (east + west))


def cells_of(message_ref, d):
    return message_ref[pl.ds(pl.multiple_of(CELL + 8 * d, 8), 8), :].astype(jnp.int32)


def keep_kernel(field_ref, dif_ref, vel_ref, give_ref, flux_ref, keep_ref, base_ref, strip_ref):
    core = lax.axis_index("sec")
    pick(flux_ref, cells_of(give_ref, 2 - 2 * core), keep_ref, 0)
    edges(core == 0, field_ref, dif_ref, vel_ref, keep_ref, LIST, keep_ref, SIDE)
    for level in range(LEV):
        for k in range(COMP):
            base_ref[k, level] = inside(field_ref[k, level], dif_ref[level], 0.5 * vel_ref[0, level], 0.5 * vel_ref[1, level])

    half, last, column = direction(core != 0)
    lane = lax.broadcasted_iota(jnp.int32, (8, LANES), 1)
    side = jnp.zeros((8, LANES), jnp.float32)
    factor = jnp.zeros((8, LANES), jnp.float32)
    strip_ref[8 : 8 + PLANES, :] = jnp.zeros((PLANES, LANES), jnp.float32)
    strip_ref[16 + PLANES :, :] = jnp.zeros((PLANES, LANES), jnp.float32)
    for level in range(1, LEV):
        across = dif_ref[level] + half * vel_ref[0, level]
        along = dif_ref[level, pl.ds(last, 1), :] + half * vel_ref[1, level, pl.ds(last, 1), :]
        for b in range(BLOCKS):
            here = ((lane >> 4) == b) & ((lane & (LEV - 1)) == level)
            factor = jnp.where(here, pull(across[8 * b : 8 * b + 8], column), factor)
        for k in range(COMP):
            at = LEV * k + level
            for b in range(BLOCKS):
                side = jnp.where(lane == PLANES * b + at, pull(base_ref[k, level, 8 * b : 8 * b + 8, :], column), side)
            strip_ref[8 + at : 9 + at, :] = base_ref[k, level, pl.ds(last, 1), :]
            strip_ref[16 + PLANES + at : 17 + PLANES + at, :] = along
    strip_ref[:8, :] = side
    strip_ref[8 + PLANES : 16 + PLANES, :] = factor


def first_inner_kernel(give_ref, near_ref, centre_ref, other_base_ref, other_centre_ref):
    dif = near_ref[COEF : COEF + ROWS, :]
    half_u = 0.5 * near_ref[COEF + ROWS : COEF + 2 * ROWS, :]
    half_v = 0.5 * near_ref[COEF + 2 * ROWS : COEF + 3 * ROWS, :]
    for k in range(COMP):
        other_base_ref[k] = inside(near_ref[SURFACE + ROWS * k : SURFACE + ROWS * k + ROWS, :], dif, half_u, half_v)
    for b in range(BLOCKS):
        own = regrid(near_ref, KEEP, 1, entries_of(give_ref), b)
        other = regrid(give_ref, KEEP, 1, entries_of(near_ref), b)
        for k in range(COMP):
            centre_ref[k, 8 * b : 8 * b + 8, :] = own[k]
            other_centre_ref[k, 8 * b : 8 * b + 8, :] = other[k]


def second_inner_kernel(field_ref, dif_ref, vel_ref, give_ref, near_ref, flux_ref, base_ref, centre_ref, list_ref):
    for level in range(LEV):
        for k in range(COMP):
            base_ref[k, level] = inside(field_ref[k, level], dif_ref[level], 0.5 * vel_ref[0, level], 0.5 * vel_ref[1, level])
    pick(flux_ref, cells_of(near_ref, 1), list_ref, 0)
    for b in range(BLOCKS):
        total = regrid(list_ref, 0, 1, entries_of(give_ref), b)
        for k in range(COMP):
            centre_ref[k, 8 * b : 8 * b + 8, :] = total[k]


def send_kernel(keep_ref, near_ref, lon_ref, lat_ref):
    lon_ref[:SIDE, :] = keep_ref[:SIDE, :]
    lon_ref[SIDE:, :] = near_ref[:SIDE, :]
    lat_ref[:PLANES, :] = keep_ref[SIDE:, :]
    lat_ref[PLANES : 2 * PLANES, :] = near_ref[SIDE:KEEP, :]


def first_turn_kernel(lon_ref, lat_ref, strip_ref, centre_ref, back_ref):
    back_ref[: 2 * SIDE, :] = lon_ref[...]
    back_ref[2 * SIDE : STRIP, :] = lat_ref[...]
    back_ref[STRIP:, :] = strip_ref[...]


def second_turn_kernel(lon_ref, lat_ref, base_ref, back_ref, edge_ref):
    back_ref[:LIST, :] = lon_ref[:LIST, :]
    back_ref[LIST:SIDE, :] = lon_ref[SIDE + LIST :, :]
    back_ref[SIDE:, :] = lat_ref[PLANES : 2 * PLANES, :]
    edge_ref[:8, :] = lon_ref[LIST:SIDE, :]
    edge_ref[8:, :] = lat_ref[:PLANES, :]


def kept(list_ref, offset, entries, centre_ref, part_ref):
    source = 2 * lax.axis_index("sec")
    for b in range(BLOCKS):
        rows = slice(8 * b, 8 * b + 8)
        total = regrid(list_ref, offset, source, entries, b)
        for k in range(COMP):
            part_ref[k, rows, :] = centre_ref[k, rows, :] + total[k]


def first_kept_kernel(give_ref, near_ref, lon_ref, centre_ref, other_centre_ref, part_ref, other_part_ref):
    kept(lon_ref, SIDE, entries_of(give_ref), centre_ref, part_ref)
    kept(lon_ref, 0, entries_of(near_ref), other_centre_ref, other_part_ref)


def second_kept_kernel(give_ref, lon_ref, centre_ref, part_ref):
    kept(lon_ref, SIDE, entries_of(give_ref), centre_ref, part_ref)


def around(core, kept_side, passed_side, kept_row, passed_row):
    first = core == 0
    from_west = jnp.where(first, kept_side, passed_side)
    from_east = jnp.where(first, passed_side, kept_side)
    lane = lax.broadcasted_iota(jnp.int32, (8, LANES), 1)
    row = lax.broadcasted_iota(jnp.int32, (8, LANES), 0)

    def arrived(k, level, b):
        at = LEV * k + level
        j = PLANES * b + at
        edge_east = jnp.broadcast_to(from_east[:, j : j + 1], (8, LANES))
        edge_west = jnp.broadcast_to(from_west[:, j : j + 1], (8, LANES))
        edge = jnp.where(lane == LANES - 1, edge_east, jnp.where(lane == 0, edge_west, 0.0))
        if b == 0 or b == BLOCKS - 1:
            pair = (kept_row(at), passed_row(at)) if b == 0 else (passed_row(at), kept_row(at))
            end = jnp.broadcast_to(jnp.where(first, *pair), (8, LANES))
            edge = edge + jnp.where(row == (0 if b == 0 else 7), end, 0.0)
        return edge

    return arrived


def finish(core, base_ref, part_ref, entries, arrived, list_ref, out_ref, ready):
    for k in range(COMP):
        for level in range(1, LEV):
            for b in range(BLOCKS):
                rows = slice(8 * b, 8 * b + 8)
                out_ref[k, level, rows, :] = base_ref[k, level, rows, :] + arrived(k, level, b)
    ready()
    for b in range(BLOCKS):
        rows = slice(8 * b, 8 * b + 8)
        total = regrid(list_ref, 0, 2 - 2 * core, entries, b)
        for k in range(COMP):
            out_ref[k, 0, rows, :] = (base_ref[k, 0, rows, :] + arrived(k, 0, b)) + (part_ref[k, rows, :] + total[k])


def other_edges(core, surface_ref, near_ref, lat_ref, lon_ref, back_ref, out_lon_ref, out_lat_ref):
    first = core == 0
    half, last, column = direction(first)
    lane = lax.broadcasted_iota(jnp.int32, (8, LANES), 1)
    row = lax.broadcasted_iota(jnp.int32, (8, LANES), 0)
    passed_side = back_ref[LIST:SIDE, :]
    kept_side = lon_ref[SIDE + LIST :, :]
    from_west = jnp.where(first, kept_side, passed_side)
    from_east = jnp.where(first, passed_side, kept_side)

    corner_north = jnp.zeros((8, LANES), jnp.float32)
    corner_south = jnp.zeros((8, LANES), jnp.float32)
    for i in range(PLANES // 8):
        passed = back_ref[2 * SIDE + 8 * i : 2 * SIDE + 8 * i + 8, :]
        kept_rows = lat_ref[PLANES + 8 * i : PLANES + 8 * i + 8, :]
        south = pull(jnp.where(first, kept_rows, passed), column)
        north = pull(jnp.where(first, passed, kept_rows), column)
        corner_south = corner_south + jnp.where(lane == row + 8 * i, south, 0.0)
        corner_north = corner_north + jnp.where(lane == row + 8 * i + PLANES * (BLOCKS - 1), north, 0.0)
        index = row + 8 * i + jnp.where(first, PLANES * (BLOCKS - 1), 0)
        end_west = jnp.where(first, from_west[7:8], from_west[0:1])
        end_east = jnp.where(first, from_east[7:8], from_east[0:1])
        west = pull(jnp.broadcast_to(end_west, (8, LANES)), index)
        east = pull(jnp.broadcast_to(end_east, (8, LANES)), index)
        ends = jnp.where(lane == LANES - 1, east, jnp.where(lane == 0, west, 0.0))
        at = STRIP + 8 + 8 * i
        line = back_ref[at : at + 8, :] + passed + ends
        factor = back_ref[at + 8 + PLANES : at + 16 + PLANES, :]
        out_lat_ref[PLANES + 8 * i : PLANES + 8 * i + 8, :] = factor * line
    corner_south = jnp.broadcast_to(jnp.sum(corner_south, axis=0, keepdims=True), (8, LANES))
    corner_north = jnp.broadcast_to(jnp.sum(corner_north, axis=0, keepdims=True), (8, LANES))
    corner = jnp.where(row == 0, corner_south, jnp.where(row == 7, corner_north, 0.0))
    factor = back_ref[STRIP + 8 + PLANES : STRIP + 16 + PLANES, :]
    side = factor * (back_ref[STRIP : STRIP + 8, :] + passed_side + corner)

    across = near_ref[COEF : COEF + ROWS, :] + half * near_ref[COEF + ROWS : COEF + 2 * ROWS, :]
    along = near_ref[pl.ds(COEF + last, 1), :] + half * near_ref[pl.ds(COEF + 2 * ROWS + last, 1), :]
    for k in range(COMP):
        at = LEV * k
        product = across * surface_ref[k]
        for b in range(BLOCKS):
            side = jnp.where(lane == PLANES * b + at, pull(product[8 * b : 8 * b + 8], column), side)
        out_lat_ref[PLANES + at : PLANES + at + 1, :] = along * surface_ref[k, pl.ds(last, 1), :]
    out_lon_ref[SIDE + LIST :, :] = side


def middle_kernel(
    base_ref, part_ref, other_base_ref, other_part_ref, give_ref, near_ref, lon_ref, lat_ref, back_ref, dif_ref, vel_ref,
    out_ref, out_lon_ref, out_lat_ref, other_flux_ref, flux_ref, surface_ref,
):
    core = lax.axis_index("sec")
    arrived = around(
        core, lon_ref[LIST:SIDE, :], back_ref[SIDE + LIST : 2 * SIDE, :],
        lambda at: lat_ref[at : at + 1, :], lambda at: back_ref[2 * SIDE + PLANES + at : 2 * SIDE + PLANES + at + 1, :],
    )
    finish(core, base_ref, part_ref, entries_of(give_ref), arrived, back_ref, out_ref, lambda: None)
    arrived = around(
        core, lon_ref[SIDE + LIST :, :], back_ref[LIST:SIDE, :],
        lambda at: lat_ref[PLANES + at : PLANES + at + 1, :], lambda at: back_ref[2 * SIDE + at : 2 * SIDE + at + 1, :],
    )
    for b in range(BLOCKS):
        rows = slice(8 * b, 8 * b + 8)
        total = regrid(back_ref, SIDE, 2 - 2 * core, entries_of(near_ref), b)
        for k in range(COMP):
            surface_ref[k, rows, :] = (other_base_ref[k, rows, :] + arrived(k, 0, b)) + (other_part_ref[k, rows, :] + total[k])
    for message_ref, planes, to_ref, offset in (
        (give_ref, [out_ref[k, 0] for k in range(COMP)], flux_ref, 0),
        (near_ref, [surface_ref[k] for k in range(COMP)], other_flux_ref, SIDE),
    ):
        fluxes(planes, message_ref[SENS : SENS + COMP, :], message_ref[SEA:SLOT, :], to_ref)
        pick(to_ref, cells_of(message_ref, 2 - 2 * core), out_lon_ref, offset)
    edges(core == 0, out_ref, dif_ref, vel_ref, out_lon_ref, LIST, out_lat_ref, 0)
    other_edges(core, surface_ref, near_ref, lat_ref, lon_ref, back_ref, out_lon_ref, out_lat_ref)


def last_kernel(base_ref, part_ref, give_ref, edge_ref, back_ref, out_hbm, out_ref, sems):
    core = lax.axis_index("sec")
    deep = pltpu.make_async_copy(out_ref.at[:, pl.ds(1, LEV - 1)], out_hbm.at[:, pl.ds(1, LEV - 1)], sems.at[0])
    top = pltpu.make_async_copy(out_ref.at[:, 0], out_hbm.at[:, 0], sems.at[1])
    arrived = around(
        core, edge_ref[:8, :], back_ref[LIST:SIDE, :],
        lambda at: edge_ref[8 + at : 9 + at, :], lambda at: back_ref[SIDE + at : SIDE + at + 1, :],
    )
    finish(core, base_ref, part_ref, entries_of(give_ref), arrived, back_ref, out_ref, deep.start)
    top.start()
    deep.wait()
    top.wait()


def call(kernel, arrays, outs, scratch=(), space=pltpu.VMEM, out_space=pltpu.VMEM, cost=1 << 20):
    in_space = pl.BlockSpec(memory_space=space)
    to_space = pl.BlockSpec(memory_space=out_space)
    return pl.pallas_call(
        kernel,
        out_shape=[jax.ShapeDtypeStruct(shape, jnp.float32) for shape in outs],
        in_specs=[in_space] * len(arrays),
        out_specs=[to_space] * len(outs),
        scratch_shapes=list(scratch),
        compiler_params=pltpu.CompilerParams(vmem_limit_bytes=8 << 20),
        cost_estimate=pl.CostEstimate(flops=cost, transcendentals=0, bytes_accessed=cost),
    )(*arrays)


def routes(axis):
    count = lax.axis_size(axis)
    periodic = axis == "lon"
    pairs = []
    for i in range(count):
        if periodic or i + 1 < count:
            pairs.append((i, (i + 1) % count))
        if periodic or i > 0:
            pairs.append((count + i, count + (i - 1) % count))
    return pairs


def on_device(
    adjoint,
    diffusivity,
    velocity,
    sensitivity,
    sea_mask,
    coast_distance,
    send_cells,
    recv_slots,
    regrid_weight,
):
    field = adjoint[0]
    sens = sensitivity[0]
    dif, vel = diffusivity[0], velocity[0]
    send = (sea_mask[0], coast_distance[0], send_cells.reshape(8 * PEERS, LANES))
    take = (recv_slots[0], regrid_weight[0])
    swap = [(0, 1), (1, 0)]
    surface = (COMP, ROWS, LANES)
    lon_rows, lat_rows = (2 * SIDE, LANES), (2 * PLANES, LANES)
    fresh = (sens, field, dif, vel, *send, *take)
    held = [pltpu.VMEM(a.shape, a.dtype) for a in fresh]
    fresh = [pltpu.with_memory_space_constraint(a, pltpu.HBM) for a in fresh]
    sems = pltpu.SemaphoreType.DMA((10,))
    give, flux = call(start_kernel, fresh, [(FIRST, LANES), surface], [*held, sems], pltpu.HBM)

    near = lax.ppermute(give, "sec", swap)
    strip = (BACK - STRIP, LANES)
    keep, base, strip = call(keep_kernel, (field, dif, vel, give, flux), [(KEEP, LANES), field.shape, strip])
    lon, lat = call(send_kernel, (keep, near), [lon_rows, lat_rows])
    lon = lax.ppermute(lon, ("sec", "lon"), routes("lon"))
    lat = lax.ppermute(lat, ("sec", "lat"), routes("lat"))
    centre, other_base, other_centre = call(first_inner_kernel, (give, near), [surface] * 3)
    (back,) = call(first_turn_kernel, (lon, lat, strip, centre), [(BACK, LANES)])
    back = lax.ppermute(back, "sec", swap)
    part, other_part = call(first_kept_kernel, (give, near, lon, centre, other_centre), [surface] * 2)

    scratch = [pltpu.VMEM(surface, jnp.float32)] * 2
    field, lon, lat, flux = call(
        middle_kernel,
        (base, part, other_base, other_part, give, near, lon, lat, back, dif, vel),
        [field.shape, lon_rows, lat_rows, surface],
        scratch,
    )
    lon = lax.ppermute(lon, ("sec", "lon"), routes("lon"))
    lat = lax.ppermute(lat, ("sec", "lat"), routes("lat"))
    scratch = [pltpu.VMEM((LIST, LANES), jnp.float32)]
    base, centre = call(second_inner_kernel, (field, dif, vel, give, near, flux), [field.shape, surface], scratch)
    back, edge = call(second_turn_kernel, (lon, lat, base), [(KEEP, LANES), (8 + PLANES, LANES)])
    back = lax.ppermute(back, "sec", swap)
    (part,) = call(second_kept_kernel, (give, lon, centre), [surface])
    scratch = [pltpu.VMEM(field.shape, jnp.float32), pltpu.SemaphoreType.DMA((2,))]
    (field,) = call(last_kernel, (base, part, give, edge, back), [field.shape], scratch, out_space=pltpu.HBM)
    return field[None]


def solution(mesh):
    placed = (
        P("sec", None, None, "lat", "lon"),
        P("sec", None, "lat", "lon"),
        P("sec", None, None, "lat", "lon"),
        P("sec", None, None),
        P("sec", "lat", "lon"),
        P("sec", "lat", "lon"),
        P("sec", "lat", "lon", None),
        P("sec", None, "lat", "lon"),
        P("sec", None, "lat", "lon"),
    )
    return jax.shard_map(
        on_device,
        mesh=mesh,
        in_specs=placed,
        out_specs=P("sec", None, None, "lat", "lon"),
        check_vma=False,
    )
```

```python
import jax
import jax.numpy as jnp
from jax import lax
from jax.experimental import pallas as pl
from jax.experimental.pallas import tpu as pltpu
from jax.sharding import PartitionSpec as P

COMP = 4
LEV = 4
TERMS = 4
ROWS = 32
LANES = 128
BLOCKS = ROWS // 8
PEERS = 3
PLANES = COMP * LEV

LIST = 8 * COMP
SIDE = LIST + 8
KEEP = SIDE + PLANES
GIVE = KEEP + LIST
SURFACE = GIVE
COEF = SURFACE + COMP * ROWS
SEA = COEF + 3 * ROWS
SLOT = SEA + ROWS
WEIGHT = SLOT + TERMS * ROWS
CELL = WEIGHT + TERMS * ROWS
SENS = CELL + 8 * PEERS
FIRST = SENS + 8
STRIP = 2 * SIDE + 2 * PLANES
BACK = STRIP + 2 * (8 + PLANES)


def lookup(rows, high, low, first_row):
    found = [jnp.zeros((8, LANES), jnp.float32) for _ in range(COMP)]
    for r in range(len(rows[0])):
        here = high == first_row + r
        for k in range(COMP):
            row = jnp.broadcast_to(rows[k][r](), (8, LANES))
            got = jnp.take_along_axis(row, low, axis=1, mode="promise_in_bounds")
            found[k] = jnp.where(here, got, found[k])
    return found


def regrid(list_ref, offset, source, entries, b):
    slots, weights = entries

    def row_of(k, r):
        at = offset + 8 * k + r
        return lambda: list_ref[at : at + 1, :]

    table = [[row_of(k, r) for r in range(8)] for k in range(COMP)]
    total = None
    for t in range(TERMS):
        slot = slots(t, b)
        found = lookup(table, slot >> 7, slot & (LANES - 1), 8 * source)
        found = [weights(t, b) * entry for entry in found]
        total = found if total is None else [a + b for a, b in zip(total, found)]
    return total


def entries_of(message_ref):
    def rows(base, t, b):
        return message_ref[base + ROWS * t + 8 * b : base + ROWS * t + 8 * b + 8, :]

    return (lambda t, b: rows(SLOT, t, b).astype(jnp.int32)), (lambda t, b: rows(WEIGHT, t, b))


def fluxes(surface, sens_ref, weight, flux_ref):
    for k in range(COMP):
        total = sens_ref[k : k + 1, 0:1] * surface[0]
        for j in range(1, COMP):
            total = total + sens_ref[k : k + 1, j : j + 1] * surface[j]
        flux_ref[k] = weight * total


def pick(flux_ref, cell, out_ref, offset):
    def row_of(k, r):
        return lambda: flux_ref[k, r : r + 1, :]

    table = [[row_of(k, r) for r in range(ROWS)] for k in range(COMP)]
    found = lookup(table, cell >> 7, cell & (LANES - 1), 0)
    for k in range(COMP):
        out_ref[offset + 8 * k : offset + 8 * k + 8, :] = found[k]


def direction(upward):
    half = jnp.where(upward, -0.5, 0.5).astype(jnp.float32)
    last = jnp.where(upward, ROWS - 1, 0)
    column = jnp.broadcast_to(jnp.where(upward, LANES - 1, 0), (8, LANES))
    return half, last, column


def pull(value, index):
    return jnp.take_along_axis(value, index, axis=1, mode="promise_in_bounds")


def edges(upward, field_ref, dif_ref, vel_ref, side_ref, side_at, row_ref, row_at):
    half, last, column = direction(upward)
    lane = lax.broadcasted_iota(jnp.int32, (8, LANES), 1)
    side = jnp.zeros((8, LANES), jnp.float32)
    for level in range(LEV):
        across = dif_ref[level] + half * vel_ref[0, level]
        along = dif_ref[level, pl.ds(last, 1), :] + half * vel_ref[1, level, pl.ds(last, 1), :]
        for k in range(COMP):
            at = LEV * k + level
            product = across * field_ref[k, level]
            for b in range(BLOCKS):
                side = jnp.where(lane == PLANES * b + at, pull(product[8 * b : 8 * b + 8], column), side)
            row_ref[row_at + at : row_at + at + 1, :] = along * field_ref[k, level, pl.ds(last, 1), :]
    side_ref[side_at : side_at + 8, :] = side


def given(core, flux_ref, send_ref, give_ref):
    pick(flux_ref, send_ref[pl.ds(pl.multiple_of(16 * core, 8), 8), :], give_ref, 0)
    pick(flux_ref, send_ref[8:16, :], give_ref, KEEP)


def sea_weight(sea_ref, dist_ref):
    distance = dist_ref[...].astype(jnp.float32)
    blend = (distance + 1.0) / (distance + 9.0)
    return sea_ref[...].astype(jnp.float32) * blend


def start_kernel(
    sens_hbm, field_hbm, dif_hbm, vel_hbm, sea_hbm, dist_hbm, send_hbm, slot_hbm, weight_hbm,
    give_ref, flux_ref, sens_ref, field_ref, dif_ref, vel_ref, sea_ref, dist_ref, send_ref, slot_ref, weight_ref, sems,
):
    early = [(sens_hbm, sens_ref), (send_hbm, send_ref), (sea_hbm, sea_ref), (dist_hbm, dist_ref)]
    early += [(field_hbm.at[:, 0], field_ref.at[:, 0])]
    late = [(dif_hbm, dif_ref), (vel_hbm, vel_ref), (slot_hbm, slot_ref), (weight_hbm, weight_ref)]
    late += [(field_hbm.at[:, pl.ds(1, LEV - 1)], field_ref.at[:, pl.ds(1, LEV - 1)])]
    copies = [pltpu.make_async_copy(a, b, sems.at[i]) for i, (a, b) in enumerate(early + late)]
    for copy in copies:
        copy.start()
    for copy in copies[: len(early)]:
        copy.wait()

    core = lax.axis_index("sec")
    sea = sea_weight(sea_ref, dist_ref)
    fluxes([field_ref[k, 0] for k in range(COMP)], sens_ref, sea, flux_ref)
    given(core, flux_ref, send_ref, give_ref)
    give_ref[SEA:SLOT, :] = sea
    give_ref[CELL:SENS, :] = send_ref[...].astype(jnp.float32)
    give_ref[SENS:, :] = jnp.zeros((8, LANES), jnp.float32)
    give_ref[SENS : SENS + COMP, 0:COMP] = sens_ref[...]
    for copy in copies[len(early) :]:
        copy.wait()
    edges(core != 0, field_ref, dif_ref, vel_ref, give_ref, LIST, give_ref, SIDE)
    for k in range(COMP):
        give_ref[SURFACE + ROWS * k : SURFACE + ROWS * k + ROWS, :] = field_ref[k, 0]
    for i, plane in enumerate((dif_ref[0], vel_ref[0, 0], vel_ref[1, 0])):
        give_ref[COEF + ROWS * i : COEF + ROWS * i + ROWS, :] = plane
    for t in range(TERMS):
        give_ref[SLOT + ROWS * t : SLOT + ROWS * t + ROWS, :] = slot_ref[t].astype(jnp.float32)
        give_ref[WEIGHT + ROWS * t : WEIGHT + ROWS * t + ROWS, :] = weight_ref[t]


def inside(plane, dif, half_u, half_v):
    lane = lax.broadcasted_iota(jnp.int32, (ROWS, LANES), 1)
    row = lax.broadcasted_iota(jnp.int32, (ROWS, LANES), 0)
    east = jnp.where(lane == LANES - 1, 0.0, pltpu.roll((dif + half_u) * plane, LANES - 1, 1))
    west = jnp.where(lane == 0, 0.0, pltpu.roll((dif - half_u) * plane, 1, 1))
    north = jnp.where(row == ROWS - 1, 0.0, pltpu.roll((dif + half_v) * plane, ROWS - 1, 0))
    south = jnp.where(row == 0, 0.0, pltpu.roll((dif - half_v) * plane, 1, 0))
    return plane - 4.0 * (dif * plane) + ((north + south) + (east + west))


def cells_of(message_ref, d):
    return message_ref[pl.ds(pl.multiple_of(CELL + 8 * d, 8), 8), :].astype(jnp.int32)


def strip_of(upward, base_ref, dif_ref, vel_ref, strip_ref):
    half, last, column = direction(upward)
    lane = lax.broadcasted_iota(jnp.int32, (8, LANES), 1)
    side = jnp.zeros((8, LANES), jnp.float32)
    factor = jnp.zeros((8, LANES), jnp.float32)
    strip_ref[8 : 8 + PLANES, :] = jnp.zeros((PLANES, LANES), jnp.float32)
    strip_ref[16 + PLANES :, :] = jnp.zeros((PLANES, LANES), jnp.float32)
    for level in range(1, LEV):
        across = dif_ref[level] + half * vel_ref[0, level]
        along = dif_ref[level, pl.ds(last, 1), :] + half * vel_ref[1, level, pl.ds(last, 1), :]
        for b in range(BLOCKS):
            here = ((lane >> 4) == b) & ((lane & (LEV - 1)) == level)
            factor = jnp.where(here, pull(across[8 * b : 8 * b + 8], column), factor)
        for k in range(COMP):
            at = LEV * k + level
            for b in range(BLOCKS):
                side = jnp.where(lane == PLANES * b + at, pull(base_ref[k, level, 8 * b : 8 * b + 8, :], column), side)
            strip_ref[8 + at : 9 + at, :] = base_ref[k, level, pl.ds(last, 1), :]
            strip_ref[16 + PLANES + at : 17 + PLANES + at, :] = along
    strip_ref[:8, :] = side
    strip_ref[8 + PLANES : 16 + PLANES, :] = factor


def keep_kernel(field_ref, dif_ref, vel_ref, give_ref, flux_ref, keep_ref, base_ref, own_strip_ref, strip_ref):
    core = lax.axis_index("sec")
    pick(flux_ref, cells_of(give_ref, 2 - 2 * core), keep_ref, 0)
    edges(core == 0, field_ref, dif_ref, vel_ref, keep_ref, LIST, keep_ref, SIDE)
    for level in range(LEV):
        for k in range(COMP):
            base_ref[k, level] = inside(field_ref[k, level], dif_ref[level], 0.5 * vel_ref[0, level], 0.5 * vel_ref[1, level])

    strip_of(core == 0, base_ref, dif_ref, vel_ref, own_strip_ref)
    strip_of(core != 0, base_ref, dif_ref, vel_ref, strip_ref)


def first_inner_kernel(give_ref, near_ref, centre_ref, other_base_ref, other_centre_ref):
    dif = near_ref[COEF : COEF + ROWS, :]
    half_u = 0.5 * near_ref[COEF + ROWS : COEF + 2 * ROWS, :]
    half_v = 0.5 * near_ref[COEF + 2 * ROWS : COEF + 3 * ROWS, :]
    for k in range(COMP):
        other_base_ref[k] = inside(near_ref[SURFACE + ROWS * k : SURFACE + ROWS * k + ROWS, :], dif, half_u, half_v)
    for b in range(BLOCKS):
        own = regrid(near_ref, KEEP, 1, entries_of(give_ref), b)
        other = regrid(give_ref, KEEP, 1, entries_of(near_ref), b)
        for k in range(COMP):
            centre_ref[k, 8 * b : 8 * b + 8, :] = own[k]
            other_centre_ref[k, 8 * b : 8 * b + 8, :] = other[k]


def second_inner_kernel(
    before_ref, surface_ref, dif_ref, vel_ref, give_ref, near_ref, flux_ref, lon_ref, lat_ref, back_ref, base_ref, centre_ref,
    field_ref, list_ref,
):
    arrived = around(
        lax.axis_index("sec"), lon_ref[LIST:SIDE, :], back_ref[SIDE + LIST : 2 * SIDE, :],
        lambda at: lat_ref[at : at + 1, :], lambda at: back_ref[2 * SIDE + PLANES + at : 2 * SIDE + PLANES + at + 1, :],
    )
    for k in range(COMP):
        for level in range(1, LEV):
            for b in range(BLOCKS):
                rows = slice(8 * b, 8 * b + 8)
                field_ref[k, level, rows, :] = before_ref[k, level, rows, :] + arrived(k, level, b)
    for level in range(LEV):
        for k in range(COMP):
            plane = surface_ref[k] if level == 0 else field_ref[k, level]
            base_ref[k, level] = inside(plane, dif_ref[level], 0.5 * vel_ref[0, level], 0.5 * vel_ref[1, level])
    pick(flux_ref, cells_of(near_ref, 1), list_ref, 0)
    for b in range(BLOCKS):
        total = regrid(list_ref, 0, 1, entries_of(give_ref), b)
        for k in range(COMP):
            centre_ref[k, 8 * b : 8 * b + 8, :] = total[k]


def send_kernel(keep_ref, near_ref, lon_ref, lat_ref):
    lon_ref[:SIDE, :] = keep_ref[:SIDE, :]
    lon_ref[SIDE:, :] = near_ref[:SIDE, :]
    lat_ref[:PLANES, :] = keep_ref[SIDE:, :]
    lat_ref[PLANES : 2 * PLANES, :] = near_ref[SIDE:KEEP, :]


def first_turn_kernel(lon_ref, lat_ref, strip_ref, centre_ref, back_ref):
    back_ref[: 2 * SIDE, :] = lon_ref[...]
    back_ref[2 * SIDE : STRIP, :] = lat_ref[...]
    back_ref[STRIP:, :] = strip_ref[...]


def second_turn_kernel(lon_ref, lat_ref, base_ref, back_ref, edge_ref):
    back_ref[:LIST, :] = lon_ref[:LIST, :]
    back_ref[LIST:SIDE, :] = lon_ref[SIDE + LIST :, :]
    back_ref[SIDE:, :] = lat_ref[PLANES : 2 * PLANES, :]
    edge_ref[:8, :] = lon_ref[LIST:SIDE, :]
    edge_ref[8:, :] = lat_ref[:PLANES, :]


def kept(list_ref, offset, entries, centre_ref, part_ref):
    source = 2 * lax.axis_index("sec")
    for b in range(BLOCKS):
        rows = slice(8 * b, 8 * b + 8)
        total = regrid(list_ref, offset, source, entries, b)
        for k in range(COMP):
            part_ref[k, rows, :] = centre_ref[k, rows, :] + total[k]


def first_kept_kernel(give_ref, near_ref, lon_ref, centre_ref, other_centre_ref, part_ref, other_part_ref):
    kept(lon_ref, SIDE, entries_of(give_ref), centre_ref, part_ref)
    kept(lon_ref, 0, entries_of(near_ref), other_centre_ref, other_part_ref)


def second_kept_kernel(give_ref, lon_ref, centre_ref, part_ref):
    kept(lon_ref, SIDE, entries_of(give_ref), centre_ref, part_ref)


def around(core, kept_side, passed_side, kept_row, passed_row):
    first = core == 0
    from_west = jnp.where(first, kept_side, passed_side)
    from_east = jnp.where(first, passed_side, kept_side)
    lane = lax.broadcasted_iota(jnp.int32, (8, LANES), 1)
    row = lax.broadcasted_iota(jnp.int32, (8, LANES), 0)

    def arrived(k, level, b):
        at = LEV * k + level
        j = PLANES * b + at
        edge_east = jnp.broadcast_to(from_east[:, j : j + 1], (8, LANES))
        edge_west = jnp.broadcast_to(from_west[:, j : j + 1], (8, LANES))
        edge = jnp.where(lane == LANES - 1, edge_east, jnp.where(lane == 0, edge_west, 0.0))
        if b == 0 or b == BLOCKS - 1:
            pair = (kept_row(at), passed_row(at)) if b == 0 else (passed_row(at), kept_row(at))
            end = jnp.broadcast_to(jnp.where(first, *pair), (8, LANES))
            edge = edge + jnp.where(row == (0 if b == 0 else 7), end, 0.0)
        return edge

    return arrived


def finish(core, base_ref, part_ref, entries, arrived, list_ref, out_ref, ready):
    for k in range(COMP):
        for level in range(1, LEV):
            for b in range(BLOCKS):
                rows = slice(8 * b, 8 * b + 8)
                out_ref[k, level, rows, :] = base_ref[k, level, rows, :] + arrived(k, level, b)
    ready()
    for b in range(BLOCKS):
        rows = slice(8 * b, 8 * b + 8)
        total = regrid(list_ref, 0, 2 - 2 * core, entries, b)
        for k in range(COMP):
            out_ref[k, 0, rows, :] = (base_ref[k, 0, rows, :] + arrived(k, 0, b)) + (part_ref[k, rows, :] + total[k])


def surface_edges(
    core, surface_ref, message_ref, kept_side, passed_side, kept_rows_of, passed_rows_of, strip_rows_of,
    out_lon_ref, lon_at, out_lat_ref, lat_at,
):
    first = core == 0
    half, last, column = direction(first)
    lane = lax.broadcasted_iota(jnp.int32, (8, LANES), 1)
    row = lax.broadcasted_iota(jnp.int32, (8, LANES), 0)
    from_west = jnp.where(first, kept_side, passed_side)
    from_east = jnp.where(first, passed_side, kept_side)

    corner_north = jnp.zeros((8, LANES), jnp.float32)
    corner_south = jnp.zeros((8, LANES), jnp.float32)
    for i in range(PLANES // 8):
        passed = passed_rows_of(8 * i, 8)
        kept_rows = kept_rows_of(8 * i, 8)
        south = pull(jnp.where(first, kept_rows, passed), column)
        north = pull(jnp.where(first, passed, kept_rows), column)
        corner_south = corner_south + jnp.where(lane == row + 8 * i, south, 0.0)
        corner_north = corner_north + jnp.where(lane == row + 8 * i + PLANES * (BLOCKS - 1), north, 0.0)
        index = row + 8 * i + jnp.where(first, PLANES * (BLOCKS - 1), 0)
        end_west = jnp.where(first, from_west[7:8], from_west[0:1])
        end_east = jnp.where(first, from_east[7:8], from_east[0:1])
        west = pull(jnp.broadcast_to(end_west, (8, LANES)), index)
        east = pull(jnp.broadcast_to(end_east, (8, LANES)), index)
        ends = jnp.where(lane == LANES - 1, east, jnp.where(lane == 0, west, 0.0))
        line = strip_rows_of(8 + 8 * i, 8) + passed + ends
        factor = strip_rows_of(16 + PLANES + 8 * i, 8)
        out_lat_ref[lat_at + 8 * i : lat_at + 8 * i + 8, :] = factor * line
    corner_south = jnp.broadcast_to(jnp.sum(corner_south, axis=0, keepdims=True), (8, LANES))
    corner_north = jnp.broadcast_to(jnp.sum(corner_north, axis=0, keepdims=True), (8, LANES))
    corner = jnp.where(row == 0, corner_south, jnp.where(row == 7, corner_north, 0.0))
    side = strip_rows_of(8 + PLANES, 8) * (strip_rows_of(0, 8) + passed_side + corner)

    across = message_ref[COEF : COEF + ROWS, :] + half * message_ref[COEF + ROWS : COEF + 2 * ROWS, :]
    along = message_ref[pl.ds(COEF + last, 1), :] + half * message_ref[pl.ds(COEF + 2 * ROWS + last, 1), :]
    for k in range(COMP):
        at = LEV * k
        product = across * surface_ref[k]
        for b in range(BLOCKS):
            side = jnp.where(lane == PLANES * b + at, pull(product[8 * b : 8 * b + 8], column), side)
        out_lat_ref[lat_at + at : lat_at + at + 1, :] = along * surface_ref[k, pl.ds(last, 1), :]
    out_lon_ref[lon_at : lon_at + 8, :] = side


def rows_from(ref, offset):
    return lambda at, count=1: ref[offset + at : offset + at + count, :]


def middle_kernel(
    base_ref, part_ref, other_base_ref, other_part_ref, own_strip_ref, give_ref, near_ref, lon_ref, lat_ref, back_ref,
    surface_ref, out_lon_ref, out_lat_ref, other_flux_ref, flux_ref, other_surface_ref,
):
    core = lax.axis_index("sec")
    sections = (
        (
            lambda k, b: base_ref[k, 0, 8 * b : 8 * b + 8, :], part_ref, give_ref, 0, lon_ref[LIST:SIDE, :],
            back_ref[SIDE + LIST : 2 * SIDE, :], rows_from(lat_ref, 0), rows_from(back_ref, 2 * SIDE + PLANES),
            rows_from(own_strip_ref, 0), surface_ref, flux_ref,
        ),
        (
            lambda k, b: other_base_ref[k, 8 * b : 8 * b + 8, :], other_part_ref, near_ref, 1, lon_ref[SIDE + LIST :, :],
            back_ref[LIST:SIDE, :], rows_from(lat_ref, PLANES), rows_from(back_ref, 2 * SIDE),
            rows_from(back_ref, STRIP), other_surface_ref, other_flux_ref,
        ),
    )
    for base, part, message_ref, at, kept_side, passed_side, kept_rows, passed_rows, strip, to_ref, to_flux_ref in sections:
        arrived = around(core, kept_side, passed_side, kept_rows, passed_rows)
        for b in range(BLOCKS):
            rows = slice(8 * b, 8 * b + 8)
            total = regrid(back_ref, SIDE * at, 2 - 2 * core, entries_of(message_ref), b)
            for k in range(COMP):
                to_ref[k, rows, :] = (base(k, b) + arrived(k, 0, b)) + (part[k, rows, :] + total[k])
        planes = [to_ref[k] for k in range(COMP)]
        fluxes(planes, message_ref[SENS : SENS + COMP, :], message_ref[SEA:SLOT, :], to_flux_ref)
        pick(to_flux_ref, cells_of(message_ref, 2 - 2 * core), out_lon_ref, SIDE * at)
        surface_edges(
            core, to_ref, message_ref, kept_side, passed_side, kept_rows, passed_rows, strip,
            out_lon_ref, SIDE * at + LIST, out_lat_ref, PLANES * at,
        )


def last_kernel(base_ref, part_ref, give_ref, edge_ref, back_ref, out_hbm, out_ref, sems):
    core = lax.axis_index("sec")
    deep = pltpu.make_async_copy(out_ref.at[:, pl.ds(1, LEV - 1)], out_hbm.at[:, pl.ds(1, LEV - 1)], sems.at[0])
    top = pltpu.make_async_copy(out_ref.at[:, 0], out_hbm.at[:, 0], sems.at[1])
    arrived = around(
        core, edge_ref[:8, :], back_ref[LIST:SIDE, :],
        lambda at: edge_ref[8 + at : 9 + at, :], lambda at: back_ref[SIDE + at : SIDE + at + 1, :],
    )
    finish(core, base_ref, part_ref, entries_of(give_ref), arrived, back_ref, out_ref, deep.start)
    top.start()
    deep.wait()
    top.wait()


def call(kernel, arrays, outs, scratch=(), space=pltpu.VMEM, out_space=pltpu.VMEM, cost=1 << 20):
    in_space = pl.BlockSpec(memory_space=space)
    to_space = pl.BlockSpec(memory_space=out_space)
    return pl.pallas_call(
        kernel,
        out_shape=[jax.ShapeDtypeStruct(shape, jnp.float32) for shape in outs],
        in_specs=[in_space] * len(arrays),
        out_specs=[to_space] * len(outs),
        scratch_shapes=list(scratch),
        compiler_params=pltpu.CompilerParams(vmem_limit_bytes=8 << 20),
        cost_estimate=pl.CostEstimate(flops=cost, transcendentals=0, bytes_accessed=cost),
    )(*arrays)


def routes(axis):
    count = lax.axis_size(axis)
    periodic = axis == "lon"
    pairs = []
    for i in range(count):
        if periodic or i + 1 < count:
            pairs.append((i, (i + 1) % count))
        if periodic or i > 0:
            pairs.append((count + i, count + (i - 1) % count))
    return pairs


def on_device(
    adjoint,
    diffusivity,
    velocity,
    sensitivity,
    sea_mask,
    coast_distance,
    send_cells,
    recv_slots,
    regrid_weight,
):
    field = adjoint[0]
    sens = sensitivity[0]
    dif, vel = diffusivity[0], velocity[0]
    send = (sea_mask[0], coast_distance[0], send_cells.reshape(8 * PEERS, LANES))
    take = (recv_slots[0], regrid_weight[0])
    swap = [(0, 1), (1, 0)]
    surface = (COMP, ROWS, LANES)
    lon_rows, lat_rows = (2 * SIDE, LANES), (2 * PLANES, LANES)
    fresh = (sens, field, dif, vel, *send, *take)
    held = [pltpu.VMEM(a.shape, a.dtype) for a in fresh]
    fresh = [pltpu.with_memory_space_constraint(a, pltpu.HBM) for a in fresh]
    sems = pltpu.SemaphoreType.DMA((10,))
    give, flux = call(start_kernel, fresh, [(FIRST, LANES), surface], [*held, sems], pltpu.HBM)

    near = lax.ppermute(give, "sec", swap)
    strip = (BACK - STRIP, LANES)
    keep, base, own_strip, strip = call(
        keep_kernel, (field, dif, vel, give, flux), [(KEEP, LANES), field.shape, strip, strip]
    )
    lon, lat = call(send_kernel, (keep, near), [lon_rows, lat_rows])
    lon = lax.ppermute(lon, ("sec", "lon"), routes("lon"))
    lat = lax.ppermute(lat, ("sec", "lat"), routes("lat"))
    centre, other_base, other_centre = call(first_inner_kernel, (give, near), [surface] * 3)
    (back,) = call(first_turn_kernel, (lon, lat, strip, centre), [(BACK, LANES)])
    back = lax.ppermute(back, "sec", swap)
    part, other_part = call(first_kept_kernel, (give, near, lon, centre, other_centre), [surface] * 2)

    scratch = [pltpu.VMEM(surface, jnp.float32)] * 2
    arrived = (lon, lat, back)
    top, lon, lat, flux = call(
        middle_kernel,
        (base, part, other_base, other_part, own_strip, give, near, *arrived),
        [surface, lon_rows, lat_rows, surface],
        scratch,
    )
    lon = lax.ppermute(lon, ("sec", "lon"), routes("lon"))
    lat = lax.ppermute(lat, ("sec", "lat"), routes("lat"))
    scratch = [pltpu.VMEM(field.shape, jnp.float32), pltpu.VMEM((LIST, LANES), jnp.float32)]
    base, centre = call(
        second_inner_kernel, (base, top, dif, vel, give, near, flux, *arrived), [field.shape, surface], scratch
    )
    back, edge = call(second_turn_kernel, (lon, lat, base), [(KEEP, LANES), (8 + PLANES, LANES)])
    back = lax.ppermute(back, "sec", swap)
    (part,) = call(second_kept_kernel, (give, lon, centre), [surface])
    scratch = [pltpu.VMEM(field.shape, jnp.float32), pltpu.SemaphoreType.DMA((2,))]
    (field,) = call(last_kernel, (base, part, give, edge, back), [field.shape], scratch, out_space=pltpu.HBM)
    return field[None]


def solution(mesh):
    placed = (
        P("sec", None, None, "lat", "lon"),
        P("sec", None, "lat", "lon"),
        P("sec", None, None, "lat", "lon"),
        P("sec", None, None),
        P("sec", "lat", "lon"),
        P("sec", "lat", "lon"),
        P("sec", "lat", "lon", None),
        P("sec", None, "lat", "lon"),
        P("sec", None, "lat", "lon"),
    )
    return jax.shard_map(
        on_device,
        mesh=mesh,
        in_specs=placed,
        out_specs=P("sec", None, None, "lat", "lon"),
        check_vma=False,
    )
```

```python
import jax
import jax.numpy as jnp
from jax import lax
from jax.experimental import pallas as pl
from jax.experimental.pallas import tpu as pltpu
from jax.sharding import PartitionSpec as P

COMP = 4
LEV = 4
TERMS = 4
ROWS = 32
LANES = 128
BLOCKS = ROWS // 8
PEERS = 3
PLANES = COMP * LEV

LIST = 8 * COMP
SIDE = LIST + 8
KEEP = SIDE + PLANES
GIVE = KEEP + LIST
SURFACE = GIVE
COEF = SURFACE + COMP * ROWS
SEA = COEF + 3 * ROWS
SLOT = SEA + ROWS
WEIGHT = SLOT + TERMS * ROWS
CELL = WEIGHT + TERMS * ROWS
SENS = CELL + 8 * PEERS
FIRST = SENS + 8
STRIP = 2 * SIDE + 2 * PLANES
BACK = STRIP + 2 * (8 + PLANES)
SUMS = COMP * ROWS


def lookup(rows, high, low, first_row):
    found = [jnp.zeros((8, LANES), jnp.float32) for _ in range(COMP)]
    for r in range(len(rows[0])):
        here = high == first_row + r
        for k in range(COMP):
            row = jnp.broadcast_to(rows[k][r](), (8, LANES))
            got = jnp.take_along_axis(row, low, axis=1, mode="promise_in_bounds")
            found[k] = jnp.where(here, got, found[k])
    return found


def regrid(list_ref, offset, source, entries, b):
    slots, weights = entries

    def row_of(k, r):
        at = offset + 8 * k + r
        return lambda: list_ref[at : at + 1, :]

    table = [[row_of(k, r) for r in range(8)] for k in range(COMP)]
    total = None
    for t in range(TERMS):
        slot = slots(t, b)
        found = lookup(table, slot >> 7, slot & (LANES - 1), 8 * source)
        found = [weights(t, b) * entry for entry in found]
        total = found if total is None else [a + b for a, b in zip(total, found)]
    return total


def entries_of(message_ref):
    def rows(base, t, b):
        return message_ref[base + ROWS * t + 8 * b : base + ROWS * t + 8 * b + 8, :]

    return (lambda t, b: rows(SLOT, t, b).astype(jnp.int32)), (lambda t, b: rows(WEIGHT, t, b))


def fluxes(surface, sens_ref, weight, flux_ref):
    for k in range(COMP):
        total = sens_ref[k : k + 1, 0:1] * surface[0]
        for j in range(1, COMP):
            total = total + sens_ref[k : k + 1, j : j + 1] * surface[j]
        flux_ref[k] = weight * total


def pick(flux_ref, cell, out_ref, offset):
    def row_of(k, r):
        return lambda: flux_ref[k, r : r + 1, :]

    table = [[row_of(k, r) for r in range(ROWS)] for k in range(COMP)]
    found = lookup(table, cell >> 7, cell & (LANES - 1), 0)
    for k in range(COMP):
        out_ref[offset + 8 * k : offset + 8 * k + 8, :] = found[k]


def direction(upward):
    half = jnp.where(upward, -0.5, 0.5).astype(jnp.float32)
    last = jnp.where(upward, ROWS - 1, 0)
    column = jnp.broadcast_to(jnp.where(upward, LANES - 1, 0), (8, LANES))
    return half, last, column


def pull(value, index):
    return jnp.take_along_axis(value, index, axis=1, mode="promise_in_bounds")


def edges(upward, field_ref, dif_ref, vel_ref, side_ref, side_at, row_ref, row_at):
    half, last, column = direction(upward)
    lane = lax.broadcasted_iota(jnp.int32, (8, LANES), 1)
    side = jnp.zeros((8, LANES), jnp.float32)
    for level in range(LEV):
        across = dif_ref[level] + half * vel_ref[0, level]
        along = dif_ref[level, pl.ds(last, 1), :] + half * vel_ref[1, level, pl.ds(last, 1), :]
        for k in range(COMP):
            at = LEV * k + level
            product = across * field_ref[k, level]
            for b in range(BLOCKS):
                side = jnp.where(lane == PLANES * b + at, pull(product[8 * b : 8 * b + 8], column), side)
            row_ref[row_at + at : row_at + at + 1, :] = along * field_ref[k, level, pl.ds(last, 1), :]
    side_ref[side_at : side_at + 8, :] = side


def given(core, flux_ref, send_ref, give_ref):
    pick(flux_ref, send_ref[pl.ds(pl.multiple_of(16 * core, 8), 8), :], give_ref, 0)
    pick(flux_ref, send_ref[8:16, :], give_ref, KEEP)


def sea_weight(sea_ref, dist_ref):
    distance = dist_ref[...].astype(jnp.float32)
    blend = (distance + 1.0) / (distance + 9.0)
    return sea_ref[...].astype(jnp.float32) * blend


def start_kernel(
    sens_hbm, field_hbm, dif_hbm, vel_hbm, sea_hbm, dist_hbm, send_hbm, slot_hbm, weight_hbm,
    give_ref, flux_ref, sens_ref, field_ref, dif_ref, vel_ref, sea_ref, dist_ref, send_ref, slot_ref, weight_ref, sems,
):
    early = [(sens_hbm, sens_ref), (send_hbm, send_ref), (sea_hbm, sea_ref), (dist_hbm, dist_ref)]
    early += [(field_hbm.at[:, 0], field_ref.at[:, 0])]
    late = [(dif_hbm, dif_ref), (vel_hbm, vel_ref), (slot_hbm, slot_ref), (weight_hbm, weight_ref)]
    late += [(field_hbm.at[:, pl.ds(1, LEV - 1)], field_ref.at[:, pl.ds(1, LEV - 1)])]
    copies = [pltpu.make_async_copy(a, b, sems.at[i]) for i, (a, b) in enumerate(early + late)]
    for copy in copies:
        copy.start()
    for copy in copies[: len(early)]:
        copy.wait()

    core = lax.axis_index("sec")
    sea = sea_weight(sea_ref, dist_ref)
    fluxes([field_ref[k, 0] for k in range(COMP)], sens_ref, sea, flux_ref)
    given(core, flux_ref, send_ref, give_ref)
    give_ref[SEA:SLOT, :] = sea
    give_ref[CELL:SENS, :] = send_ref[...].astype(jnp.float32)
    give_ref[SENS:, :] = jnp.zeros((8, LANES), jnp.float32)
    give_ref[SENS : SENS + COMP, 0:COMP] = sens_ref[...]
    for copy in copies[len(early) :]:
        copy.wait()
    edges(core != 0, field_ref, dif_ref, vel_ref, give_ref, LIST, give_ref, SIDE)
    for k in range(COMP):
        give_ref[SURFACE + ROWS * k : SURFACE + ROWS * k + ROWS, :] = field_ref[k, 0]
    for i, plane in enumerate((dif_ref[0], vel_ref[0, 0], vel_ref[1, 0])):
        give_ref[COEF + ROWS * i : COEF + ROWS * i + ROWS, :] = plane
    for t in range(TERMS):
        give_ref[SLOT + ROWS * t : SLOT + ROWS * t + ROWS, :] = slot_ref[t].astype(jnp.float32)
        give_ref[WEIGHT + ROWS * t : WEIGHT + ROWS * t + ROWS, :] = weight_ref[t]


def inside(plane, dif, half_u, half_v):
    lane = lax.broadcasted_iota(jnp.int32, (ROWS, LANES), 1)
    row = lax.broadcasted_iota(jnp.int32, (ROWS, LANES), 0)
    east = jnp.where(lane == LANES - 1, 0.0, pltpu.roll((dif + half_u) * plane, LANES - 1, 1))
    west = jnp.where(lane == 0, 0.0, pltpu.roll((dif - half_u) * plane, 1, 1))
    north = jnp.where(row == ROWS - 1, 0.0, pltpu.roll((dif + half_v) * plane, ROWS - 1, 0))
    south = jnp.where(row == 0, 0.0, pltpu.roll((dif - half_v) * plane, 1, 0))
    return plane - 4.0 * (dif * plane) + ((north + south) + (east + west))


def cells_of(message_ref, d):
    return message_ref[pl.ds(pl.multiple_of(CELL + 8 * d, 8), 8), :].astype(jnp.int32)


def strip_of(upward, base_ref, dif_ref, vel_ref, strip_ref):
    half, last, column = direction(upward)
    lane = lax.broadcasted_iota(jnp.int32, (8, LANES), 1)
    side = jnp.zeros((8, LANES), jnp.float32)
    factor = jnp.zeros((8, LANES), jnp.float32)
    strip_ref[8 : 8 + PLANES, :] = jnp.zeros((PLANES, LANES), jnp.float32)
    strip_ref[16 + PLANES :, :] = jnp.zeros((PLANES, LANES), jnp.float32)
    for level in range(1, LEV):
        across = dif_ref[level] + half * vel_ref[0, level]
        along = dif_ref[level, pl.ds(last, 1), :] + half * vel_ref[1, level, pl.ds(last, 1), :]
        for b in range(BLOCKS):
            here = ((lane >> 4) == b) & ((lane & (LEV - 1)) == level)
            factor = jnp.where(here, pull(across[8 * b : 8 * b + 8], column), factor)
        for k in range(COMP):
            at = LEV * k + level
            for b in range(BLOCKS):
                side = jnp.where(lane == PLANES * b + at, pull(base_ref[k, level, 8 * b : 8 * b + 8, :], column), side)
            strip_ref[8 + at : 9 + at, :] = base_ref[k, level, pl.ds(last, 1), :]
            strip_ref[16 + PLANES + at : 17 + PLANES + at, :] = along
    strip_ref[:8, :] = side
    strip_ref[8 + PLANES : 16 + PLANES, :] = factor


def keep_kernel(field_ref, dif_ref, vel_ref, give_ref, flux_ref, keep_ref, base_ref, own_strip_ref, strip_ref):
    core = lax.axis_index("sec")
    pick(flux_ref, cells_of(give_ref, 2 - 2 * core), keep_ref, 0)
    edges(core == 0, field_ref, dif_ref, vel_ref, keep_ref, LIST, keep_ref, SIDE)
    for level in range(LEV):
        for k in range(COMP):
            base_ref[k, level] = inside(field_ref[k, level], dif_ref[level], 0.5 * vel_ref[0, level], 0.5 * vel_ref[1, level])

    strip_of(core == 0, base_ref, dif_ref, vel_ref, own_strip_ref)
    strip_of(core != 0, base_ref, dif_ref, vel_ref, strip_ref)


def first_inner_kernel(give_ref, near_ref, centre_ref, other_base_ref, other_centre_ref):
    dif = near_ref[COEF : COEF + ROWS, :]
    half_u = 0.5 * near_ref[COEF + ROWS : COEF + 2 * ROWS, :]
    half_v = 0.5 * near_ref[COEF + 2 * ROWS : COEF + 3 * ROWS, :]
    for k in range(COMP):
        other_base_ref[k] = inside(near_ref[SURFACE + ROWS * k : SURFACE + ROWS * k + ROWS, :], dif, half_u, half_v)
    for b in range(BLOCKS):
        own = regrid(near_ref, KEEP, 1, entries_of(give_ref), b)
        other = regrid(give_ref, KEEP, 1, entries_of(near_ref), b)
        for k in range(COMP):
            centre_ref[k, 8 * b : 8 * b + 8, :] = own[k]
            other_centre_ref[k, 8 * b : 8 * b + 8, :] = other[k]


def second_inner_kernel(
    before_ref, surface_ref, dif_ref, vel_ref, give_ref, near_ref, flux_ref, lon_ref, lat_ref, back_ref, base_ref, centre_ref,
    field_ref, list_ref,
):
    arrived = around(
        lax.axis_index("sec"), lon_ref[LIST:SIDE, :], back_ref[SIDE + LIST : 2 * SIDE, :],
        lambda at: lat_ref[at : at + 1, :], lambda at: back_ref[2 * SIDE + PLANES + at : 2 * SIDE + PLANES + at + 1, :],
    )
    for k in range(COMP):
        for level in range(1, LEV):
            for b in range(BLOCKS):
                rows = slice(8 * b, 8 * b + 8)
                field_ref[k, level, rows, :] = before_ref[k, level, rows, :] + arrived(k, level, b)
    for level in range(LEV):
        for k in range(COMP):
            plane = surface_ref[k] if level == 0 else field_ref[k, level]
            base_ref[k, level] = inside(plane, dif_ref[level], 0.5 * vel_ref[0, level], 0.5 * vel_ref[1, level])
    pick(flux_ref, cells_of(near_ref, 1), list_ref, 0)
    for b in range(BLOCKS):
        total = regrid(list_ref, 0, 1, entries_of(give_ref), b)
        for k in range(COMP):
            centre_ref[k, 8 * b : 8 * b + 8, :] = total[k]


def send_kernel(keep_ref, near_ref, lon_ref, lat_ref):
    lon_ref[:SIDE, :] = keep_ref[:SIDE, :]
    lon_ref[SIDE:, :] = near_ref[:SIDE, :]
    lat_ref[:PLANES, :] = keep_ref[SIDE:, :]
    lat_ref[PLANES : 2 * PLANES, :] = near_ref[SIDE:KEEP, :]


def first_turn_kernel(lon_ref, lat_ref, strip_ref, centre_ref, back_ref):
    back_ref[: 2 * SIDE, :] = lon_ref[...]
    back_ref[2 * SIDE : STRIP, :] = lat_ref[...]
    back_ref[STRIP:, :] = strip_ref[...]


def passed_kernel(near_ref, lon_ref, sum_ref):
    source = 2 * lax.axis_index("sec")
    for b in range(BLOCKS):
        total = regrid(lon_ref, 0, source, entries_of(near_ref), b)
        for k in range(COMP):
            at = ROWS * k + 8 * b
            sum_ref[at : at + 8, :] = total[k]
    sum_ref[SUMS:, :] = lon_ref[SIDE + LIST :, :]


def second_turn_kernel(sum_ref, lon_ref, lat_ref, base_ref, back_ref, edge_ref):
    back_ref[: SUMS + 8, :] = sum_ref[...]
    back_ref[SUMS + 8 :, :] = lat_ref[PLANES : 2 * PLANES, :]
    edge_ref[:8, :] = lon_ref[LIST:SIDE, :]
    edge_ref[8:, :] = lat_ref[:PLANES, :]


def kept(list_ref, offset, entries, centre_ref, part_ref):
    source = 2 * lax.axis_index("sec")
    for b in range(BLOCKS):
        rows = slice(8 * b, 8 * b + 8)
        total = regrid(list_ref, offset, source, entries, b)
        for k in range(COMP):
            part_ref[k, rows, :] = centre_ref[k, rows, :] + total[k]


def first_kept_kernel(give_ref, near_ref, lon_ref, centre_ref, other_centre_ref, part_ref, other_part_ref):
    kept(lon_ref, SIDE, entries_of(give_ref), centre_ref, part_ref)
    kept(lon_ref, 0, entries_of(near_ref), other_centre_ref, other_part_ref)


def second_kept_kernel(give_ref, lon_ref, centre_ref, part_ref):
    kept(lon_ref, SIDE, entries_of(give_ref), centre_ref, part_ref)


def around(core, kept_side, passed_side, kept_row, passed_row):
    first = core == 0
    from_west = jnp.where(first, kept_side, passed_side)
    from_east = jnp.where(first, passed_side, kept_side)
    lane = lax.broadcasted_iota(jnp.int32, (8, LANES), 1)
    row = lax.broadcasted_iota(jnp.int32, (8, LANES), 0)

    def arrived(k, level, b):
        at = LEV * k + level
        j = PLANES * b + at
        edge_east = jnp.broadcast_to(from_east[:, j : j + 1], (8, LANES))
        edge_west = jnp.broadcast_to(from_west[:, j : j + 1], (8, LANES))
        edge = jnp.where(lane == LANES - 1, edge_east, jnp.where(lane == 0, edge_west, 0.0))
        if b == 0 or b == BLOCKS - 1:
            pair = (kept_row(at), passed_row(at)) if b == 0 else (passed_row(at), kept_row(at))
            end = jnp.broadcast_to(jnp.where(first, *pair), (8, LANES))
            edge = edge + jnp.where(row == (0 if b == 0 else 7), end, 0.0)
        return edge

    return arrived


def surface_edges(
    core, surface_ref, message_ref, kept_side, passed_side, kept_rows_of, passed_rows_of, strip_rows_of,
    out_lon_ref, lon_at, out_lat_ref, lat_at,
):
    first = core == 0
    half, last, column = direction(first)
    lane = lax.broadcasted_iota(jnp.int32, (8, LANES), 1)
    row = lax.broadcasted_iota(jnp.int32, (8, LANES), 0)
    from_west = jnp.where(first, kept_side, passed_side)
    from_east = jnp.where(first, passed_side, kept_side)

    corner_north = jnp.zeros((8, LANES), jnp.float32)
    corner_south = jnp.zeros((8, LANES), jnp.float32)
    for i in range(PLANES // 8):
        passed = passed_rows_of(8 * i, 8)
        kept_rows = kept_rows_of(8 * i, 8)
        south = pull(jnp.where(first, kept_rows, passed), column)
        north = pull(jnp.where(first, passed, kept_rows), column)
        corner_south = corner_south + jnp.where(lane == row + 8 * i, south, 0.0)
        corner_north = corner_north + jnp.where(lane == row + 8 * i + PLANES * (BLOCKS - 1), north, 0.0)
        index = row + 8 * i + jnp.where(first, PLANES * (BLOCKS - 1), 0)
        end_west = jnp.where(first, from_west[7:8], from_west[0:1])
        end_east = jnp.where(first, from_east[7:8], from_east[0:1])
        west = pull(jnp.broadcast_to(end_west, (8, LANES)), index)
        east = pull(jnp.broadcast_to(end_east, (8, LANES)), index)
        ends = jnp.where(lane == LANES - 1, east, jnp.where(lane == 0, west, 0.0))
        line = strip_rows_of(8 + 8 * i, 8) + passed + ends
        factor = strip_rows_of(16 + PLANES + 8 * i, 8)
        out_lat_ref[lat_at + 8 * i : lat_at + 8 * i + 8, :] = factor * line
    corner_south = jnp.broadcast_to(jnp.sum(corner_south, axis=0, keepdims=True), (8, LANES))
    corner_north = jnp.broadcast_to(jnp.sum(corner_north, axis=0, keepdims=True), (8, LANES))
    corner = jnp.where(row == 0, corner_south, jnp.where(row == 7, corner_north, 0.0))
    side = strip_rows_of(8 + PLANES, 8) * (strip_rows_of(0, 8) + passed_side + corner)

    across = message_ref[COEF : COEF + ROWS, :] + half * message_ref[COEF + ROWS : COEF + 2 * ROWS, :]
    along = message_ref[pl.ds(COEF + last, 1), :] + half * message_ref[pl.ds(COEF + 2 * ROWS + last, 1), :]
    for k in range(COMP):
        at = LEV * k
        product = across * surface_ref[k]
        for b in range(BLOCKS):
            side = jnp.where(lane == PLANES * b + at, pull(product[8 * b : 8 * b + 8], column), side)
        out_lat_ref[lat_at + at : lat_at + at + 1, :] = along * surface_ref[k, pl.ds(last, 1), :]
    out_lon_ref[lon_at : lon_at + 8, :] = side


def rows_from(ref, offset):
    return lambda at, count=1: ref[offset + at : offset + at + count, :]


def middle_kernel(
    base_ref, part_ref, other_base_ref, other_part_ref, own_strip_ref, give_ref, near_ref, lon_ref, lat_ref, back_ref,
    surface_ref, out_lon_ref, out_lat_ref, other_flux_ref, flux_ref, other_surface_ref,
):
    core = lax.axis_index("sec")
    sections = (
        (
            lambda k, b: base_ref[k, 0, 8 * b : 8 * b + 8, :], part_ref, give_ref, 0, lon_ref[LIST:SIDE, :],
            back_ref[SIDE + LIST : 2 * SIDE, :], rows_from(lat_ref, 0), rows_from(back_ref, 2 * SIDE + PLANES),
            rows_from(own_strip_ref, 0), surface_ref, flux_ref,
        ),
        (
            lambda k, b: other_base_ref[k, 8 * b : 8 * b + 8, :], other_part_ref, near_ref, 1, lon_ref[SIDE + LIST :, :],
            back_ref[LIST:SIDE, :], rows_from(lat_ref, PLANES), rows_from(back_ref, 2 * SIDE),
            rows_from(back_ref, STRIP), other_surface_ref, other_flux_ref,
        ),
    )
    for base, part, message_ref, at, kept_side, passed_side, kept_rows, passed_rows, strip, to_ref, to_flux_ref in sections:
        arrived = around(core, kept_side, passed_side, kept_rows, passed_rows)
        for b in range(BLOCKS):
            rows = slice(8 * b, 8 * b + 8)
            total = regrid(back_ref, SIDE * at, 2 - 2 * core, entries_of(message_ref), b)
            for k in range(COMP):
                to_ref[k, rows, :] = (base(k, b) + arrived(k, 0, b)) + (part[k, rows, :] + total[k])
        planes = [to_ref[k] for k in range(COMP)]
        fluxes(planes, message_ref[SENS : SENS + COMP, :], message_ref[SEA:SLOT, :], to_flux_ref)
        pick(to_flux_ref, cells_of(message_ref, 2 - 2 * core), out_lon_ref, SIDE * at)
        surface_edges(
            core, to_ref, message_ref, kept_side, passed_side, kept_rows, passed_rows, strip,
            out_lon_ref, SIDE * at + LIST, out_lat_ref, PLANES * at,
        )


def last_kernel(base_ref, part_ref, edge_ref, back_ref, out_hbm, out_ref, sems):
    core = lax.axis_index("sec")
    arrived = around(
        core, edge_ref[:8, :], back_ref[SUMS : SUMS + 8, :],
        lambda at: edge_ref[8 + at : 9 + at, :], lambda at: back_ref[SUMS + 8 + at : SUMS + 9 + at, :],
    )
    copies = [pltpu.make_async_copy(out_ref.at[k], out_hbm.at[k], sems.at[k]) for k in range(COMP)]
    for k in range(COMP):
        for level in range(LEV):
            for b in range(BLOCKS):
                rows = slice(8 * b, 8 * b + 8)
                value = base_ref[k, level, rows, :] + arrived(k, level, b)
                if level == 0:
                    at = ROWS * k + 8 * b
                    value = value + (part_ref[k, rows, :] + back_ref[at : at + 8, :])
                out_ref[k, level, rows, :] = value
        copies[k].start()
    for copy in copies:
        copy.wait()


def call(kernel, arrays, outs, scratch=(), space=pltpu.VMEM, out_space=pltpu.VMEM, cost=1 << 20):
    in_space = pl.BlockSpec(memory_space=space)
    to_space = pl.BlockSpec(memory_space=out_space)
    return pl.pallas_call(
        kernel,
        out_shape=[jax.ShapeDtypeStruct(shape, jnp.float32) for shape in outs],
        in_specs=[in_space] * len(arrays),
        out_specs=[to_space] * len(outs),
        scratch_shapes=list(scratch),
        compiler_params=pltpu.CompilerParams(vmem_limit_bytes=8 << 20),
        cost_estimate=pl.CostEstimate(flops=cost, transcendentals=0, bytes_accessed=cost),
    )(*arrays)


def routes(axis):
    count = lax.axis_size(axis)
    periodic = axis == "lon"
    pairs = []
    for i in range(count):
        if periodic or i + 1 < count:
            pairs.append((i, (i + 1) % count))
        if periodic or i > 0:
            pairs.append((count + i, count + (i - 1) % count))
    return pairs


def on_device(
    adjoint,
    diffusivity,
    velocity,
    sensitivity,
    sea_mask,
    coast_distance,
    send_cells,
    recv_slots,
    regrid_weight,
):
    field = adjoint[0]
    sens = sensitivity[0]
    dif, vel = diffusivity[0], velocity[0]
    send = (sea_mask[0], coast_distance[0], send_cells.reshape(8 * PEERS, LANES))
    take = (recv_slots[0], regrid_weight[0])
    swap = [(0, 1), (1, 0)]
    surface = (COMP, ROWS, LANES)
    lon_rows, lat_rows = (2 * SIDE, LANES), (2 * PLANES, LANES)
    fresh = (sens, field, dif, vel, *send, *take)
    held = [pltpu.VMEM(a.shape, a.dtype) for a in fresh]
    fresh = [pltpu.with_memory_space_constraint(a, pltpu.HBM) for a in fresh]
    sems = pltpu.SemaphoreType.DMA((10,))
    give, flux = call(start_kernel, fresh, [(FIRST, LANES), surface], [*held, sems], pltpu.HBM)

    near = lax.ppermute(give, "sec", swap)
    strip = (BACK - STRIP, LANES)
    keep, base, own_strip, strip = call(
        keep_kernel, (field, dif, vel, give, flux), [(KEEP, LANES), field.shape, strip, strip]
    )
    lon, lat = call(send_kernel, (keep, near), [lon_rows, lat_rows])
    lon = lax.ppermute(lon, ("sec", "lon"), routes("lon"))
    lat = lax.ppermute(lat, ("sec", "lat"), routes("lat"))
    centre, other_base, other_centre = call(first_inner_kernel, (give, near), [surface] * 3)
    (back,) = call(first_turn_kernel, (lon, lat, strip, centre), [(BACK, LANES)])
    back = lax.ppermute(back, "sec", swap)
    part, other_part = call(first_kept_kernel, (give, near, lon, centre, other_centre), [surface] * 2)

    scratch = [pltpu.VMEM(surface, jnp.float32)] * 2
    arrived = (lon, lat, back)
    top, lon, lat, flux = call(
        middle_kernel,
        (base, part, other_base, other_part, own_strip, give, near, *arrived),
        [surface, lon_rows, lat_rows, surface],
        scratch,
    )
    lon = lax.ppermute(lon, ("sec", "lon"), routes("lon"))
    lat = lax.ppermute(lat, ("sec", "lat"), routes("lat"))
    scratch = [pltpu.VMEM(field.shape, jnp.float32), pltpu.VMEM((LIST, LANES), jnp.float32)]
    base, centre = call(
        second_inner_kernel, (base, top, dif, vel, give, near, flux, *arrived), [field.shape, surface], scratch
    )
    (sums,) = call(passed_kernel, (near, lon), [(SUMS + 8, LANES)])
    back, edge = call(second_turn_kernel, (sums, lon, lat, base), [(SUMS + 8 + PLANES, LANES), (8 + PLANES, LANES)])
    back = lax.ppermute(back, "sec", swap)
    (part,) = call(second_kept_kernel, (give, lon, centre), [surface])
    scratch = [pltpu.VMEM(field.shape, jnp.float32), pltpu.SemaphoreType.DMA((COMP,))]
    (field,) = call(last_kernel, (base, part, edge, back), [field.shape], scratch, out_space=pltpu.HBM)
    return field[None]


def solution(mesh):
    placed = (
        P("sec", None, None, "lat", "lon"),
        P("sec", None, "lat", "lon"),
        P("sec", None, None, "lat", "lon"),
        P("sec", None, None),
        P("sec", "lat", "lon"),
        P("sec", "lat", "lon"),
        P("sec", "lat", "lon", None),
        P("sec", None, "lat", "lon"),
        P("sec", None, "lat", "lon"),
    )
    return jax.shard_map(
        on_device,
        mesh=mesh,
        in_specs=placed,
        out_specs=P("sec", None, None, "lat", "lon"),
        check_vma=False,
    )
```
